32 devices in a mesh: shard: 16 (over z, x, core), rep: 2 (over y).
Axes of the slice: x: 2, y: 2, z: 4, core: 2. Of those that a mesh axis runs over, the one named last changes fastest.
Arguments:
- frames: bfloat16 [32, 256, 768], P(('shard', 'rep')), may hold values from -6 to 6
- cotangent: bfloat16 [32, 256, 768], P(('shard', 'rep')), may hold values from -6 to 6
- first_gain: bfloat16 [768], P('shard'), may hold values from 0.5 to 1.5
- first_shift: bfloat16 [768], P('shard'), may hold values from -1.75 to 1.75
- query_weight: bfloat16 [768, 768], P('shard'), may hold values from -0.21875 to 0.21875
- query_bias: bfloat16 [768], P('shard'), may hold values from -1.75 to 1.75
- key_weight: bfloat16 [768, 768], P('shard'), may hold values from -0.21875 to 0.21875
- value_weight: bfloat16 [768, 768], P('shard'), may hold values from -0.21875 to 0.21875
- value_bias: bfloat16 [768], P('shard'), may hold values from -1.75 to 1.75
- output_weight: bfloat16 [768, 768], P('shard'), may hold values from -0.4375 to 0.4375
- output_bias: bfloat16 [768], P('shard'), may hold values from -1.75 to 1.75
- second_gain: bfloat16 [768], P('shard'), may hold values from 0.5 to 1.5
- second_shift: bfloat16 [768], P('shard'), may hold values from -1.75 to 1.75
- inner_weight: bfloat16 [768, 3072], P('shard'), may hold values from -0.21875 to 0.21875
- inner_bias: bfloat16 [3072], P('shard'), may hold values from -1.75 to 1.75
- outer_weight: bfloat16 [3072, 768], P('shard'), may hold values from -0.109375 to 0.109375
- outer_bias: bfloat16 [768], P('shard'), may hold values from -1.75 to 1.75
Outputs:
- result: bfloat16 [32, 256, 768], P(('shard', 'rep'))
- input_grad: bfloat16 [32, 256, 768], P(('shard', 'rep'))
- grad_first_gain: float32 [768], P('shard')
- grad_first_shift: float32 [768], P('shard')
- grad_query_weight: float32 [768, 768], P('shard')
- grad_query_bias: float32 [768], P('shard')
- grad_key_weight: float32 [768, 768], P('shard')
- grad_value_weight: float32 [768, 768], P('shard')
- grad_value_bias: float32 [768], P('shard')
- grad_output_weight: float32 [768, 768], P('shard')
- grad_output_bias: float32 [768], P('shard')
- grad_second_gain: float32 [768], P('shard')
- grad_second_shift: float32 [768], P('shard')
- grad_inner_weight: float32 [768, 3072], P('shard')
- grad_inner_bias: float32 [3072], P('shard')
- grad_outer_weight: float32 [3072, 768], P('shard')
- grad_outer_bias: float32 [768], P('shard')
The draws below stay inside these ranges and needn't reach their ends.
All inputs are finite; a program needn't handle non-finite values.
Results may differ from the reference program's by a relative error of at most 0.019.
Values may be sent and summed in bfloat16 or wider, within the bound.
A program may use at most 128 MiB of HBM per device.

```python
import jax
import jax.numpy as jnp
from jax import lax

D = 768
HEADS = 12
HD = 64
FF = 3072
FRAMES = 256
CLIPS = 32


def with_spikes(values, rng, source, target, blocks, factor):
    def block_of(position):
        return (jnp.arange(values.shape[position]) // (values.shape[position] // blocks)).reshape((-1,) + (1,) * (values.ndim - 1 - position))

    one_side = jax.random.permutation(rng, blocks)[block_of(target)]
    other_side = (block_of(target) + blocks // 2) % blocks
    return jnp.where((block_of(source) == one_side) | (block_of(source) == other_side), factor * values, values)


def levels(key, extent, pieces, smallest, high):
    def one(axis_at, blocks):
        steps = jax.random.uniform(jax.random.fold_in(jax.random.fold_in(key, 6), axis_at), (blocks,), jnp.float32, smallest / len(pieces), high / len(pieces))
        return jnp.repeat(jnp.exp(steps), extent[axis_at] // blocks).reshape((-1,) + (1,) * (len(extent) - axis_at - 1))

    loudness = one(*pieces[0])
    for cut in pieces[1:]:
        loudness = loudness * one(*cut)
    return loudness


def centred(own_key, extent, width, bound, split=(), held_as=jnp.bfloat16):
    drawn = width * jax.random.normal(own_key, extent, jnp.float32)
    if split:
        drawn = drawn * levels(own_key, extent, split, -0.22, 0.18)
    return jnp.clip(drawn, -bound, bound).astype(held_as)


def bell_draw_with(own_key, shape, scale, reach, split, heavy, held_as=jnp.bfloat16):
    entries = scale * jax.random.normal(own_key, shape, jnp.float32)
    if split:
        entries = entries * levels(own_key, shape, split, -0.22, 0.18)
    return jnp.clip(with_spikes(entries, jax.random.fold_in(own_key, 3), *heavy), -reach, reach).astype(held_as)


def setup_inputs(seed: int = 0) -> dict:
    streams_of = jax.random.split(jax.random.key(seed), 18)
    return {
        "frames": bell_draw_with(streams_of[0], (CLIPS, FRAMES, D), 1.0, 6.0, ((0, 32),), (0, 2, 32, 2.75)),
        "cotangent": centred(streams_of[1], (CLIPS, FRAMES, D), 1.0, 6.0, ((0, 32),)),
        "first_gain": jnp.clip(1.0 + 0.1 * jax.random.normal(streams_of[2], (D,), jnp.float32), 0.5, 1.5).astype(jnp.bfloat16),
        "first_shift": centred(streams_of[3], (D,), 0.3, 1.75, ((0, 16),)),
        "query_weight": centred(streams_of[4], (D, D), D ** -0.5, 0.21875, ((0, 16),)),
        "query_bias": centred(streams_of[5], (D,), 0.3, 1.75, ((0, 16),)),
        "key_weight": centred(streams_of[6], (D, D), D ** -0.5, 0.21875, ((0, 16),)),
        "value_weight": centred(streams_of[7], (D, D), D ** -0.5, 0.21875, ((0, 16),)),
        "value_bias": centred(streams_of[8], (D,), 0.3, 1.75, ((0, 16),)),
        "output_weight": centred(streams_of[9], (D, D), (D // 4) ** -0.5, 0.4375, ((0, 16),)),
        "output_bias": centred(streams_of[10], (D,), 0.3, 1.75, ((0, 16),)),
        "second_gain": jnp.clip(1.0 + 0.1 * jax.random.normal(streams_of[11], (D,), jnp.float32), 0.5, 1.5).astype(jnp.bfloat16),
        "second_shift": centred(streams_of[12], (D,), 0.3, 1.75, ((0, 16),)),
        "inner_weight": centred(streams_of[13], (D, FF), D ** -0.5, 0.21875, ((0, 16),)),
        "inner_bias": centred(streams_of[14], (FF,), 0.3, 1.75, ((0, 16),)),
        "outer_weight": centred(streams_of[15], (FF, D), FF ** -0.5, 0.109375, ((0, 16),)),
        "outer_bias": centred(streams_of[16], (D,), 0.3, 1.75, ((0, 16),)),
    }


EPSILON = 1e-05

def normalize(values, gain, shift):
    center = lax.optimization_barrier(jnp.mean(values, axis=-1, keepdims=True))
    spread = lax.optimization_barrier(jnp.mean((values - center) ** 2, axis=-1, keepdims=True))
    inv_std = lax.rsqrt(spread + EPSILON)
    normed = (values - center) * inv_std
    return (normed * gain.astype(jnp.float32) + shift.astype(jnp.float32), normed, inv_std)

def norm_back(grad_out, normed, inv_std, gain):
    scaled = grad_out * gain.astype(jnp.float32)
    return inv_std * (scaled - lax.optimization_barrier(jnp.mean(scaled, axis=-1, keepdims=True)) - normed * lax.optimization_barrier(jnp.mean(scaled * normed, axis=-1, keepdims=True)))

def gelu_parts(inner):
    cdf = 0.5 * (1.0 + jax.scipy.special.erf(inner * 0.7071067811865476))
    density = jnp.exp(-0.5 * inner * inner) * 0.3989422804014327
    return (inner * cdf, cdf + inner * density)

def heads_of(matrix):
    return matrix.reshape(matrix.shape[0], HEADS, HD).astype(jnp.float32)

def matmul(left, right):
    return jnp.dot(left, right, preferred_element_type=jnp.float32)

def forward_clip(clip, params):
    first_gain, first_shift, query_weight, query_bias, key_weight, value_weight, value_bias, output_weight, output_bias, second_gain, second_shift, inner_weight, inner_bias, outer_weight, outer_bias = params
    start = clip.astype(jnp.float32)
    normed_one, hat_one, inv_one = normalize(start, first_gain, first_shift)
    first_low = normed_one.astype(jnp.bfloat16)
    query = ((matmul(first_low, query_weight) + query_bias.astype(jnp.float32)) * HD ** (-0.5)).astype(jnp.bfloat16)
    keys = matmul(first_low, key_weight).astype(jnp.bfloat16)
    values = (matmul(first_low, value_weight) + value_bias.astype(jnp.float32)).astype(jnp.bfloat16)
    scores = jnp.einsum('qhd,khd->hqk', heads_of(query), heads_of(keys))
    highest = lax.optimization_barrier(jnp.max(scores, axis=-1, keepdims=True))
    log_total = highest + jnp.log(lax.optimization_barrier(jnp.sum(jnp.exp(scores - highest), axis=-1, keepdims=True)))
    probs = jnp.exp(scores - log_total).astype(jnp.bfloat16)
    context = jnp.einsum('hqk,khd->qhd', probs.astype(jnp.float32), heads_of(values)).reshape(-1, D).astype(jnp.bfloat16)
    mixed = start + matmul(context, output_weight) + output_bias.astype(jnp.float32)
    normed_two, hat_two, inv_two = normalize(mixed, second_gain, second_shift)
    second_low = normed_two.astype(jnp.bfloat16)
    inner = matmul(second_low, inner_weight) + inner_bias.astype(jnp.float32)
    active, slope = gelu_parts(inner)
    active_low = active.astype(jnp.bfloat16)
    result = (mixed + matmul(active_low, outer_weight) + outer_bias.astype(jnp.float32)).astype(jnp.bfloat16)
    saved = (hat_one, inv_one, first_low, query, keys, values, log_total, context, hat_two, inv_two, second_low, slope, active_low)
    return (result, saved)

def backward_clip(grad_low, saved, params):
    first_gain, first_shift, query_weight, query_bias, key_weight, value_weight, value_bias, output_weight, output_bias, second_gain, second_shift, inner_weight, inner_bias, outer_weight, outer_bias = params
    hat_one, inv_one, first_low, query, keys, values, log_total, context, hat_two, inv_two, second_low, slope, active_low = saved
    grad = grad_low.astype(jnp.float32)
    g_outer_bias = lax.optimization_barrier(jnp.sum(grad, axis=0))
    g_outer = matmul(active_low.T, grad_low)
    d_inner = matmul(grad_low, outer_weight.T) * slope
    d_inner_low = d_inner.astype(jnp.bfloat16)
    g_inner_bias = lax.optimization_barrier(jnp.sum(d_inner, axis=0))
    g_inner = matmul(second_low.T, d_inner_low)
    d_second = matmul(d_inner_low, inner_weight.T)
    g_second_gain = lax.optimization_barrier(jnp.sum(d_second * hat_two, axis=0))
    g_second_shift = lax.optimization_barrier(jnp.sum(d_second, axis=0))
    d_mixed = grad + norm_back(d_second, hat_two, inv_two, second_gain)
    d_mixed_low = d_mixed.astype(jnp.bfloat16)
    g_output_bias = lax.optimization_barrier(jnp.sum(d_mixed, axis=0))
    g_output = matmul(context.T, d_mixed_low)
    d_context = matmul(d_mixed_low, output_weight.T).astype(jnp.bfloat16)
    query_heads = heads_of(query)
    keys_heads = heads_of(keys)
    values_heads = heads_of(values)
    dctx_heads = heads_of(d_context)
    scores = jnp.einsum('qhd,khd->hqk', query_heads, keys_heads)
    probs = jnp.exp(scores - log_total)
    probs_low = probs.astype(jnp.bfloat16).astype(jnp.float32)
    d_probs = jnp.einsum('qhd,khd->hqk', dctx_heads, values_heads)
    delta = lax.optimization_barrier(jnp.sum(dctx_heads * heads_of(context), axis=-1))
    d_scores = (probs * (d_probs - jnp.transpose(delta)[:, :, None])).astype(jnp.bfloat16).astype(jnp.float32)
    d_values = jnp.einsum('hqk,qhd->khd', probs_low, dctx_heads).reshape(-1, D)
    d_query = jnp.einsum('hqk,khd->qhd', d_scores, keys_heads).reshape(-1, D) * HD ** (-0.5)
    d_keys = jnp.einsum('hqk,qhd->khd', d_scores, query_heads).reshape(-1, D)
    dq_low = d_query.astype(jnp.bfloat16)
    dk_low = d_keys.astype(jnp.bfloat16)
    dv_low = d_values.astype(jnp.bfloat16)
    g_query_bias = lax.optimization_barrier(jnp.sum(d_query, axis=0))
    g_value_bias = lax.optimization_barrier(jnp.sum(d_values, axis=0))
    g_query = matmul(first_low.T, dq_low)
    g_keys = matmul(first_low.T, dk_low)
    g_values = matmul(first_low.T, dv_low)
    d_first = matmul(dq_low, query_weight.T) + matmul(dk_low, key_weight.T) + matmul(dv_low, value_weight.T)
    g_first_gain = lax.optimization_barrier(jnp.sum(d_first * hat_one, axis=0))
    g_first_shift = lax.optimization_barrier(jnp.sum(d_first, axis=0))
    d_start = (d_mixed + norm_back(d_first, hat_one, inv_one, first_gain)).astype(jnp.bfloat16)
    grads = (g_first_gain, g_first_shift, g_query, g_query_bias, g_keys, g_values, g_value_bias, g_output, g_output_bias, g_second_gain, g_second_shift, g_inner, g_inner_bias, g_outer, g_outer_bias)
    return (d_start, grads)

def reference(frames, cotangent, first_gain, first_shift, query_weight, query_bias, key_weight, value_weight, value_bias, output_weight, output_bias, second_gain, second_shift, inner_weight, inner_bias, outer_weight, outer_bias):
    params = (first_gain, first_shift, query_weight, query_bias, key_weight, value_weight, value_bias, output_weight, output_bias, second_gain, second_shift, inner_weight, inner_bias, outer_weight, outer_bias)

    def one_clip(totals, pair):
        clip, grad_low = pair
        result, saved = forward_clip(clip, params)
        d_start, grads = backward_clip(grad_low, saved, params)
        return (tuple((total + piece for total, piece in zip(totals, grads))), (result, d_start))
    zeros = tuple((jnp.zeros(weight.shape, jnp.float32) for weight in params))
    totals, (results, input_grad) = lax.scan(one_clip, zeros, (frames, cotangent))
    return (results, input_grad, totals[0], totals[1], totals[2], totals[3], totals[4], totals[5], totals[6], totals[7], totals[8], totals[9], totals[10], totals[11], totals[12], totals[13], totals[14])
```

```python
import functools

import jax
import jax.numpy as jnp
from jax import lax
from jax.experimental import pallas as pl
from jax.experimental.pallas import tpu as pltpu
from jax.sharding import PartitionSpec as P

D = 768
HEADS = 12
HD = 64


EPSILON = 1e-05


def normalize(values, gain, shift):
    center = jnp.mean(values, axis=-1, keepdims=True)
    spread = jnp.mean((values - center) ** 2, axis=-1, keepdims=True)
    inv_std = lax.rsqrt(spread + EPSILON)
    normed = (values - center) * inv_std
    return (normed * gain.astype(jnp.float32) + shift.astype(jnp.float32), normed, inv_std)


def norm_back(grad_out, normed, inv_std, gain):
    scaled = grad_out * gain.astype(jnp.float32)
    return inv_std * (
        scaled
        - jnp.mean(scaled, axis=-1, keepdims=True)
        - normed * jnp.mean(scaled * normed, axis=-1, keepdims=True)
    )


def gelu_parts(inner):
    cdf = 0.5 * (1.0 + jax.scipy.special.erf(inner * 0.7071067811865476))
    density = jnp.exp(-0.5 * inner * inner) * 0.3989422804014327
    return (inner * cdf, cdf + inner * density)


def heads_of(matrix):
    return matrix.reshape(matrix.shape[0], HEADS, HD)


def matmul(left, right):
    return jnp.dot(left, right, preferred_element_type=jnp.float32)


def forward_clip(clip, params):
    (
        first_gain,
        first_shift,
        query_weight,
        query_bias,
        key_weight,
        value_weight,
        value_bias,
        output_weight,
        output_bias,
        second_gain,
        second_shift,
        inner_weight,
        inner_bias,
        outer_weight,
        outer_bias,
    ) = params
    start = clip.astype(jnp.float32)
    normed_one, hat_one, inv_one = normalize(start, first_gain, first_shift)
    first_low = normed_one.astype(jnp.bfloat16)
    query = (
        (matmul(first_low, query_weight) + query_bias.astype(jnp.float32)) * HD ** (-0.5)
    ).astype(jnp.bfloat16)
    keys = matmul(first_low, key_weight).astype(jnp.bfloat16)
    values = (matmul(first_low, value_weight) + value_bias.astype(jnp.float32)).astype(jnp.bfloat16)
    scores = jnp.einsum(
        "qhd,khd->hqk", heads_of(query), heads_of(keys), preferred_element_type=jnp.float32
    )
    highest = jnp.max(scores, axis=-1, keepdims=True)
    log_total = highest + jnp.log(jnp.sum(jnp.exp(scores - highest), axis=-1, keepdims=True))
    probs = jnp.exp(scores - log_total).astype(jnp.bfloat16)
    context = (
        jnp.einsum("hqk,khd->qhd", probs, heads_of(values), preferred_element_type=jnp.float32)
        .reshape(-1, D)
        .astype(jnp.bfloat16)
    )
    mixed = start + matmul(context, output_weight) + output_bias.astype(jnp.float32)
    normed_two, hat_two, inv_two = normalize(mixed, second_gain, second_shift)
    second_low = normed_two.astype(jnp.bfloat16)
    inner = matmul(second_low, inner_weight) + inner_bias.astype(jnp.float32)
    active, slope = gelu_parts(inner)
    active_low = active.astype(jnp.bfloat16)
    result = (mixed + matmul(active_low, outer_weight) + outer_bias.astype(jnp.float32)).astype(
        jnp.bfloat16
    )
    saved = (
        hat_one,
        inv_one,
        first_low,
        query,
        keys,
        values,
        log_total,
        context,
        hat_two,
        inv_two,
        second_low,
        slope,
        active_low,
    )
    return (result, saved)


def backward_clip(grad_low, saved, params):
    (
        first_gain,
        first_shift,
        query_weight,
        query_bias,
        key_weight,
        value_weight,
        value_bias,
        output_weight,
        output_bias,
        second_gain,
        second_shift,
        inner_weight,
        inner_bias,
        outer_weight,
        outer_bias,
    ) = params
    (
        hat_one,
        inv_one,
        first_low,
        query,
        keys,
        values,
        log_total,
        context,
        hat_two,
        inv_two,
        second_low,
        slope,
        active_low,
    ) = saved
    grad = grad_low.astype(jnp.float32)
    g_outer_bias = jnp.sum(grad, axis=0)
    g_outer = matmul(active_low.T, grad_low)
    d_inner = matmul(grad_low, outer_weight.T) * slope
    d_inner_low = d_inner.astype(jnp.bfloat16)
    g_inner_bias = jnp.sum(d_inner, axis=0)
    g_inner = matmul(second_low.T, d_inner_low)
    d_second = matmul(d_inner_low, inner_weight.T)
    g_second_gain = jnp.sum(d_second * hat_two, axis=0)
    g_second_shift = jnp.sum(d_second, axis=0)
    d_mixed = grad + norm_back(d_second, hat_two, inv_two, second_gain)
    d_mixed_low = d_mixed.astype(jnp.bfloat16)
    g_output_bias = jnp.sum(d_mixed, axis=0)
    g_output = matmul(context.T, d_mixed_low)
    d_context = matmul(d_mixed_low, output_weight.T).astype(jnp.bfloat16)
    query_heads = heads_of(query)
    keys_heads = heads_of(keys)
    values_heads = heads_of(values)
    dctx_heads = heads_of(d_context)
    scores = jnp.einsum("qhd,khd->hqk", query_heads, keys_heads, preferred_element_type=jnp.float32)
    probs = jnp.exp(scores - log_total)
    probs_low = probs.astype(jnp.bfloat16)
    d_probs = jnp.einsum(
        "qhd,khd->hqk", dctx_heads, values_heads, preferred_element_type=jnp.float32
    )
    delta = jnp.sum(dctx_heads.astype(jnp.float32) * heads_of(context).astype(jnp.float32), axis=-1)
    d_scores = (probs * (d_probs - jnp.transpose(delta)[:, :, None])).astype(jnp.bfloat16)
    d_values = jnp.einsum(
        "hqk,qhd->khd", probs_low, dctx_heads, preferred_element_type=jnp.float32
    ).reshape(-1, D)
    d_query = jnp.einsum(
        "hqk,khd->qhd", d_scores, keys_heads, preferred_element_type=jnp.float32
    ).reshape(-1, D) * HD ** (-0.5)
    d_keys = jnp.einsum(
        "hqk,qhd->khd", d_scores, query_heads, preferred_element_type=jnp.float32
    ).reshape(-1, D)
    dq_low = d_query.astype(jnp.bfloat16)
    dk_low = d_keys.astype(jnp.bfloat16)
    dv_low = d_values.astype(jnp.bfloat16)
    g_query_bias = jnp.sum(d_query, axis=0)
    g_value_bias = jnp.sum(d_values, axis=0)
    g_query = matmul(first_low.T, dq_low)
    g_keys = matmul(first_low.T, dk_low)
    g_values = matmul(first_low.T, dv_low)
    d_first = (
        matmul(dq_low, query_weight.T)
        + matmul(dk_low, key_weight.T)
        + matmul(dv_low, value_weight.T)
    )
    g_first_gain = jnp.sum(d_first * hat_one, axis=0)
    g_first_shift = jnp.sum(d_first, axis=0)
    d_start = (d_mixed + norm_back(d_first, hat_one, inv_one, first_gain)).astype(jnp.bfloat16)
    grads = (
        g_first_gain,
        g_first_shift,
        g_query,
        g_query_bias,
        g_keys,
        g_values,
        g_value_bias,
        g_output,
        g_output_bias,
        g_second_gain,
        g_second_shift,
        g_inner,
        g_inner_bias,
        g_outer,
        g_outer_bias,
    )
    return (d_start, grads)


MESH = pl.DeviceIdType.MESH


class Ring:
    def __init__(self, chips):
        self.chips = chips
        shard = lax.axis_index("shard")
        self.rep = lax.axis_index("rep")
        self.core = lax.rem(shard, 2)
        chip = shard // 2
        half = chip // 2
        self.pos = half + lax.rem(chip, 2) * (chips - 1 - 2 * half)
        self.step = 1 - 2 * self.core
        self.me = shard
        self.mate = chip * 2 + (1 - self.core)

    def shard_at(self, offset, core):
        place = lax.rem(self.pos + offset + 2 * self.chips, self.chips)
        far = place // (self.chips // 2)
        chip = (1 - far) * 2 * place + far * (2 * (self.chips - 1 - place) + 1)
        return chip * 2 + core

    def next(self):
        return self.shard_at(self.step, self.core)

    def previous(self):
        return self.shard_at(-self.step, self.core)


def rows_of(owner, rows):
    return pl.ds(pl.multiple_of(owner * rows, rows), rows)


def greet(ring, others, reps):
    barrier = pltpu.get_barrier_semaphore()
    for other in others:
        pl.semaphore_signal(barrier, inc=1, device_id=(other, ring.rep), device_id_type=MESH)
    for shift in range(1, reps):
        pl.semaphore_signal(
            barrier,
            inc=1,
            device_id=(ring.me, lax.rem(ring.rep + shift, reps)),
            device_id_type=MESH,
        )
    pl.semaphore_wait(barrier, len(others) + reps - 1)


def gather_kernel(chips, count, *refs):
    ins, outs = refs[:count], refs[count : 2 * count]
    ring_send, ring_recv, mate_send, mate_recv, own_sem = refs[2 * count :]
    ring = Ring(chips)
    core = ring.core
    following, mate = ring.next(), ring.mate
    greet(ring, (following, ring.previous(), mate), 1)

    def where(index, owner):
        return outs[index].at[rows_of(owner, ins[index].shape[0])]

    def to_next(index, step, owner, source):
        return pltpu.make_async_remote_copy(
            src_ref=source,
            dst_ref=where(index, owner),
            send_sem=ring_send.at[step, index],
            recv_sem=ring_recv.at[step, index],
            device_id=(following, ring.rep),
            device_id_type=MESH,
        )

    def to_mate(index, step, owner, source):
        return pltpu.make_async_remote_copy(
            src_ref=source,
            dst_ref=where(index, owner),
            send_sem=mate_send.at[step, index],
            recv_sem=mate_recv.at[step, index],
            device_id=(mate, ring.rep),
            device_id_type=MESH,
        )

    for index in range(count):
        to_next(index, 0, ring.me, ins[index]).start()
    for index in range(count):
        to_mate(index, 0, ring.me, ins[index]).start()
        pltpu.make_async_copy(ins[index], where(index, ring.me), own_sem.at[index]).start()

    def hop(step, carry):
        owner = ring.shard_at(-ring.step * step, core)
        for index in range(count):
            block = where(index, owner)
            to_next(index, step - 1, owner, block).wait_recv()
            pl.when(step < chips - 1)(lambda: to_next(index, step, owner, block).start())
            to_mate(index, step, owner, block).start()
        return carry

    lax.fori_loop(1, chips, hop, 0)

    def finish(step, carry):
        owner = ring.shard_at(-ring.step * step, core)
        theirs = ring.shard_at(ring.step * step, 1 - core)
        for index in range(count):
            to_mate(index, step, theirs, where(index, theirs)).wait_recv()
            to_mate(index, step, owner, where(index, owner)).wait_send()
            pl.when(step < chips - 1)(
                lambda: to_next(index, step, owner, where(index, owner)).wait_send()
            )
        return carry

    lax.fori_loop(0, chips, finish, 0)
    for index in range(count):
        pltpu.make_async_copy(ins[index], where(index, ring.me), own_sem.at[index]).wait()


def gather_all(pieces, shards):
    chips, count = shards // 2, len(pieces)
    return pl.pallas_call(
        functools.partial(gather_kernel, chips, count),
        out_shape=[
            jax.ShapeDtypeStruct((piece.shape[0] * shards, piece.shape[1]), piece.dtype)
            for piece in pieces
        ],
        in_specs=[pl.BlockSpec(memory_space=pltpu.VMEM)] * count,
        out_specs=[pl.BlockSpec(memory_space=pl.ANY)] * count,
        scratch_shapes=[
            pltpu.SemaphoreType.DMA((chips, count)),
            pltpu.SemaphoreType.DMA((chips, count)),
            pltpu.SemaphoreType.DMA((chips, count)),
            pltpu.SemaphoreType.DMA((chips, count)),
            pltpu.SemaphoreType.DMA((count,)),
        ],
        compiler_params=pltpu.CompilerParams(collective_id=0, has_side_effects=True),
        name="gather_all",
    )(*pieces)


def scatter_kernel(chips, reps, count, *refs):
    ins, outs = refs[:count], refs[count : 2 * count]
    held = refs[2 * count : 3 * count]
    arrived = refs[3 * count : 4 * count]
    peers = refs[4 * count : 5 * count]
    ring_send, ring_recv, mate_send, mate_recv, rep_send, rep_recv = refs[5 * count :]
    ring = Ring(chips)
    core = ring.core
    following, mate = ring.next(), ring.mate
    greet(ring, (following, ring.previous(), mate), reps)

    def to_mate(index, step):
        owner = ring.shard_at(ring.step * (step + 1), 1 - core)
        rows = outs[index].shape[0]
        return pltpu.make_async_remote_copy(
            src_ref=ins[index].at[rows_of(owner, rows)],
            dst_ref=held[index].at[step],
            send_sem=mate_send.at[step, index],
            recv_sem=mate_recv.at[step, index],
            device_id=(mate, ring.rep),
            device_id_type=MESH,
        )

    def to_next(index, step):
        return pltpu.make_async_remote_copy(
            src_ref=held[index].at[step],
            dst_ref=arrived[index].at[step],
            send_sem=ring_send.at[step, index],
            recv_sem=ring_recv.at[step, index],
            device_id=(following, ring.rep),
            device_id_type=MESH,
        )

    def to_rep(index, shift):
        return pltpu.make_async_remote_copy(
            src_ref=held[index].at[chips - 1],
            dst_ref=peers[index].at[ring.rep],
            send_sem=rep_send.at[shift, index],
            recv_sem=rep_recv.at[shift, index],
            device_id=(ring.me, lax.rem(ring.rep + shift, reps)),
            device_id_type=MESH,
        )

    def hand_over(step, carry):
        for index in range(count):
            to_mate(index, step).start()
        return carry

    lax.fori_loop(0, chips, hand_over, 0)

    def add(index, step, first):
        owner = ring.shard_at(-ring.step * (step + 1), core)
        rows = outs[index].shape[0]
        to_mate(index, step).wait_recv()
        total = ins[index][rows_of(owner, rows), :].astype(jnp.float32) + held[index][step].astype(
            jnp.float32
        )
        if not first:
            to_next(index, step - 1).wait_recv()
            total = total + arrived[index][step - 1].astype(jnp.float32)
        held[index][step] = total.astype(jnp.bfloat16)

    for index in range(count):
        add(index, 0, True)
        to_next(index, 0).start()

    def hop(step, carry):
        for index in range(count):
            add(index, step, False)
            to_next(index, step).start()
        return carry

    lax.fori_loop(1, chips - 1, hop, 0)
    for index in range(count):
        add(index, chips - 1, False)
        for shift in range(1, reps):
            to_rep(index, shift).start()
        peers[index][ring.rep] = held[index][chips - 1]
    for index in range(count):
        for shift in range(1, reps):
            to_rep(index, shift).wait_recv()
        total = peers[index][0].astype(jnp.float32)
        for rep in range(1, reps):
            total = total + peers[index][rep].astype(jnp.float32)
        outs[index][...] = total

    def finish(step, carry):
        for index in range(count):
            to_mate(index, step).wait_send()
            pl.when(step < chips - 1)(lambda: to_next(index, step).wait_send())
        return carry

    lax.fori_loop(0, chips, finish, 0)
    for index in range(count):
        for shift in range(1, reps):
            to_rep(index, shift).wait_send()


def scatter_all(pieces, shards, reps):
    chips, count = shards // 2, len(pieces)
    blocks = [(piece.shape[0] // shards, piece.shape[1]) for piece in pieces]
    return pl.pallas_call(
        functools.partial(scatter_kernel, chips, reps, count),
        out_shape=[jax.ShapeDtypeStruct(block, jnp.float32) for block in blocks],
        in_specs=[pl.BlockSpec(memory_space=pltpu.VMEM)] * count,
        out_specs=[pl.BlockSpec(memory_space=pltpu.VMEM)] * count,
        scratch_shapes=[pltpu.VMEM((chips,) + block, jnp.bfloat16) for block in blocks]
        + [pltpu.VMEM((chips - 1,) + block, jnp.bfloat16) for block in blocks]
        + [pltpu.VMEM((reps,) + block, jnp.bfloat16) for block in blocks]
        + [pltpu.SemaphoreType.DMA((chips, count))] * 4
        + [pltpu.SemaphoreType.DMA((reps, count))] * 2,
        compiler_params=pltpu.CompilerParams(
            collective_id=1, has_side_effects=True, vmem_limit_bytes=60 * 1024 * 1024
        ),
        name="scatter_all",
    )(*pieces)


NARROW = (0, 1, 3, 6, 8, 9, 10, 14)
WIDE = 12
WEIGHTS = (2, 4, 5, 7, 11, 13)
LANES = 128
SUBLANES = 16


def packed_rows(size):
    return -(-size // (LANES * SUBLANES)) * SUBLANES


def pack(vectors, owners):
    flat = jnp.concatenate(
        [vectors[i].reshape(owners, -1) for i in NARROW] + [vectors[WIDE].reshape(owners, -1)],
        axis=1,
    )
    rows = packed_rows(flat.shape[1])
    flat = jnp.pad(flat, ((0, 0), (0, rows * LANES - flat.shape[1])))
    return flat.reshape(owners * rows, LANES)


def unpack(block, owners, narrow, wide):
    flat = block.reshape(owners, -1)
    count = len(NARROW)
    first = flat[:, : count * narrow].reshape(owners, count, narrow)
    first = jnp.transpose(first, (1, 0, 2)).reshape(count, owners * narrow)
    found = {i: first[k] for k, i in enumerate(NARROW)}
    found[WIDE] = flat[:, count * narrow : count * narrow + wide].reshape(-1)
    return found


def per_device_plain(shards, reps, frames, cotangent, *local):
    narrow, wide = local[0].shape[0], local[WIDE].shape[0]
    gathered = gather_all([local[i] for i in WEIGHTS] + [pack(local, 1)], shards)
    params = [None] * len(local)
    for k, i in enumerate(WEIGHTS):
        params[i] = gathered[k]
    for i, vector in unpack(gathered[-1], shards, narrow, wide).items():
        params[i] = vector
    params = tuple(params)

    results, input_grads, totals = [], [], None
    for k in range(frames.shape[0]):
        result, saved = forward_clip(frames[k], params)
        d_start, grads = backward_clip(cotangent[k], saved, params)
        results.append(result)
        input_grads.append(d_start)
        totals = grads if totals is None else tuple(a + b for a, b in zip(totals, grads))

    low = [total.astype(jnp.bfloat16) for total in totals]
    summed = scatter_all([low[i] for i in WEIGHTS] + [pack(low, shards)], shards, reps)
    out = [None] * len(local)
    for k, i in enumerate(WEIGHTS):
        out[i] = summed[k]
    for i, vector in unpack(summed[-1], 1, narrow, wide).items():
        out[i] = vector
    return (jnp.stack(results), jnp.stack(input_grads), *out)


TN = (((0,), (0,)), ((), ()))
NT = (((1,), (1,)), ((), ()))
CHUNK = 256
BLOCK = 32


def dot_tn(left, right):
    return lax.dot_general(left, right, TN, preferred_element_type=jnp.float32)


def dot_nt(left, right):
    return lax.dot_general(left, right, NT, preferred_element_type=jnp.float32)


def span(start, size, unit):
    return pl.ds(pl.multiple_of(start, unit), size)


class Gather:
    def __init__(self, ring, chips, ins, outs, crossed, sems):
        self.ring, self.chips, self.ins, self.outs, self.crossed = ring, chips, ins, outs, crossed
        (
            self.ring_send,
            self.ring_recv,
            self.mate_send,
            self.mate_recv,
            self.peer_send,
            self.peer_recv,
            self.own_sem,
        ) = sems
        self.next, self.mate = ring.next(), ring.mate

    def rows(self, i):
        return self.ins[i].shape[0]

    def part(self, i, kind):
        rows, cross = self.rows(i), self.crossed[i]
        if kind == "all":
            return 0, rows
        if kind == "ringed":
            return self.ring.rep * cross, rows - cross
        if kind == "sent":
            return self.ring.rep * (rows - cross), cross
        return (1 - self.ring.rep) * (rows - cross), cross

    def remote(self, i, step, owner, kind, send, recv, target, own=False):
        offset, size = self.part(i, kind)
        place = self.outs[i].at[span(owner * self.rows(i) + offset, size, SUBLANES)]
        source = self.ins[i].at[span(offset, size, SUBLANES)] if own else place
        return pltpu.make_async_remote_copy(
            src_ref=source,
            dst_ref=place,
            send_sem=send.at[step, i],
            recv_sem=recv.at[step, i],
            device_id=target,
            device_id_type=MESH,
        )

    def to_next(self, i, step, owner, own=False):
        target = (self.next, self.ring.rep)
        return self.remote(
            i, step, owner, "ringed", self.ring_send, self.ring_recv, target, own
        )

    def to_mate(self, i, step, owner, kind, own=False):
        target = (self.mate, self.ring.rep)
        return self.remote(i, step, owner, kind, self.mate_send, self.mate_recv, target, own)

    def to_peer(self, i, step, owner, kind):
        target = (self.ring.me, 1 - self.ring.rep)
        return self.remote(i, step, owner, kind, self.peer_send, self.peer_recv, target)

    def own_copy(self, i):
        place = self.outs[i].at[span(self.ring.me * self.rows(i), self.rows(i), SUBLANES)]
        return pltpu.make_async_copy(self.ins[i], place, self.own_sem.at[i])

    def owner(self, step):
        return self.ring.shard_at(-self.ring.step * step, self.ring.core)

    def start(self, i):
        self.to_next(i, 0, self.ring.me, True).start()
        self.to_mate(i, 0, self.ring.me, "all", True).start()
        self.own_copy(i).start()

    def hop(self, i, step):
        owner = self.owner(step)
        self.to_next(i, step - 1, owner).wait_recv()
        if step < self.chips - 1:
            self.to_next(i, step, owner).start()
        if self.crossed[i]:
            self.to_peer(i, step, owner, "sent").start()
        self.to_mate(i, step, owner, "ringed").start()

    def cross(self, i, step):
        if self.crossed[i]:
            owner = self.owner(step)
            self.to_peer(i, step, owner, "got").wait_recv()
            self.to_mate(i, step, owner, "got").start()

    def finish(self, i):
        for step in range(self.chips):
            theirs = self.ring.shard_at(self.ring.step * step, 1 - self.ring.core)
            self.to_mate(i, step, theirs, "all").wait_recv()
        self.own_copy(i).wait()

    def drain(self, i):
        for step in range(self.chips):
            owner = self.owner(step)
            self.to_mate(i, step, owner, "all").wait_send()
            if step < self.chips - 1:
                self.to_next(i, step, owner).wait_send()
            if step and self.crossed[i]:
                self.to_peer(i, step, owner, "sent").wait_send()


class Scatter:
    def __init__(self, ring, chips, terms, outs, held, arrived, peers, others, crossed, sems):
        self.ring, self.chips, self.terms, self.outs = ring, chips, terms, outs
        self.held, self.arrived, self.peers, self.others = held, arrived, peers, others
        self.crossed = crossed
        (
            self.mate_send,
            self.mate_recv,
            self.ring_send,
            self.ring_recv,
            self.peer_send,
            self.peer_recv,
            self.last_send,
            self.last_recv,
        ) = sems
        self.next, self.mate = ring.next(), ring.mate

    def rows(self, i):
        return self.outs[i].shape[0]

    def spots(self, i):
        rep, rows, cross = self.ring.rep, self.rows(i), self.crossed[i]
        return {
            "ringed": rep * cross,
            "kept": rep * (rows - cross),
            "middle": cross,
            "given": (1 - rep) * (rows - cross),
            "kept_in": rep * (rows - 2 * cross),
            "middle_in": (1 - rep) * cross,
            "other_kept_in": (1 - rep) * (rows - 2 * cross),
            "other_middle_in": rep * cross,
        }

    def copy(self, source, target, send, recv, device):
        return pltpu.make_async_remote_copy(
            src_ref=source,
            dst_ref=target,
            send_sem=send,
            recv_sem=recv,
            device_id=device,
            device_id_type=MESH,
        )

    def owner(self, step):
        return self.ring.shard_at(-self.ring.step * (step + 1), self.ring.core)

    def to_mate(self, i, step):
        owner = self.ring.shard_at(self.ring.step * (step + 1), 1 - self.ring.core)
        return self.copy(
            self.terms[i].at[rows_of(owner, self.rows(i))],
            self.held[i].at[step],
            self.mate_send.at[step, i],
            self.mate_recv.at[step, i],
            (self.mate, self.ring.rep),
        )

    def to_next(self, i, step):
        size = self.rows(i) - self.crossed[i]
        return self.copy(
            self.held[i].at[step, span(self.spots(i)["ringed"], size, SUBLANES)],
            self.arrived[i].at[step],
            self.ring_send.at[step, i],
            self.ring_recv.at[step, i],
            (self.next, self.ring.rep),
        )

    def to_peer(self, i, step):
        return self.copy(
            self.held[i].at[step, span(self.spots(i)["given"], self.crossed[i], SUBLANES)],
            self.peers[i].at[step],
            self.peer_send.at[step, i],
            self.peer_recv.at[step, i],
            (self.ring.me, 1 - self.ring.rep),
        )

    def to_last(self, i):
        size = self.rows(i) - self.crossed[i]
        return self.copy(
            self.held[i].at[self.chips - 1, span(self.spots(i)["ringed"], size, SUBLANES)],
            self.others[i],
            self.last_send.at[i],
            self.last_recv.at[i],
            (self.ring.me, 1 - self.ring.rep),
        )

    def start(self, i):
        for step in range(self.chips):
            self.to_mate(i, step).start()

    def both(self, i, step, offset, size):
        mine = self.terms[i][span(self.owner(step) * self.rows(i) + offset, size, SUBLANES), :]
        theirs = self.held[i][step, span(offset, size, SUBLANES), :]
        return mine.astype(jnp.float32) + theirs.astype(jnp.float32)

    def keep(self, i, step, offset, total):
        place = span(offset, total.shape[0], SUBLANES)
        self.held[i][step, place, :] = total.astype(jnp.bfloat16)

    def give(self, i, step):
        self.to_mate(i, step).wait_recv()
        if self.crossed[i]:
            offset = self.spots(i)["given"]
            self.keep(i, step, offset, self.both(i, step, offset, self.crossed[i]))
            self.to_peer(i, step).start()

    def hop(self, i, step):
        spots, cross = self.spots(i), self.crossed[i]
        middle = self.rows(i) - 2 * cross
        if step:
            self.to_next(i, step - 1).wait_recv()
        total = self.both(i, step, spots["middle"], middle)
        if step:
            part = self.arrived[i][step - 1, span(spots["middle_in"], middle, SUBLANES), :]
            total = total + part.astype(jnp.float32)
        self.keep(i, step, spots["middle"], total)
        if cross:
            self.to_peer(i, step).wait_recv()
            total = self.both(i, step, spots["kept"], cross)
            total = total + self.peers[i][step].astype(jnp.float32)
            if step:
                part = self.arrived[i][step - 1, span(spots["kept_in"], cross, SUBLANES), :]
                total = total + part.astype(jnp.float32)
            self.keep(i, step, spots["kept"], total)
        if step < self.chips - 1:
            self.to_next(i, step).start()
        else:
            self.to_last(i).start()

    def finish(self, i):
        spots, cross = self.spots(i), self.crossed[i]
        middle, last = self.rows(i) - 2 * cross, self.chips - 1
        self.to_last(i).wait_recv()
        mine = self.held[i][last, span(spots["middle"], middle, SUBLANES), :]
        theirs = self.others[i][span(spots["other_middle_in"], middle, SUBLANES), :]
        self.outs[i][span(spots["middle"], middle, SUBLANES), :] = mine.astype(
            jnp.float32
        ) + theirs.astype(jnp.float32)
        if cross:
            kept = span(spots["kept"], cross, SUBLANES)
            self.outs[i][kept, :] = self.held[i][last, kept, :].astype(jnp.float32)
            other = self.others[i][span(spots["other_kept_in"], cross, SUBLANES), :]
            given = span(spots["given"], cross, SUBLANES)
            self.outs[i][given, :] = other.astype(jnp.float32)

    def drain(self, i):
        for step in range(self.chips):
            self.to_mate(i, step).wait_send()
            if step < self.chips - 1:
                self.to_next(i, step).wait_send()
            if self.crossed[i]:
                self.to_peer(i, step).wait_send()
        self.to_last(i).wait_send()


Q, K, V, O, INNER, OUTER, PACK = range(7)
SLOTS = 16
SPREAD = len(NARROW)
VECTOR = {name: row for row, name in enumerate(NARROW)}


def iota(shape, axis):
    return lax.broadcasted_iota(jnp.int32, shape, axis)


def one_hot(condition):
    return jnp.where(condition, 1.0, 0.0).astype(jnp.bfloat16)


def bits(size):
    return size.bit_length() - 1


def packed_slots(index, shards, ratio):
    owner, slot = index >> bits(SLOTS), index & (SLOTS - 1)
    wide = owner * ratio + slot - SPREAD
    line = jnp.where(slot < SPREAD, slot, SPREAD + (wide >> bits(shards)))
    group = jnp.where(slot < SPREAD, owner, wide & (shards - 1))
    return line, group, slot < SPREAD + ratio


def pick_table(shards, ratio):
    shape = (SLOTS, shards * SLOTS)
    line, _, used = packed_slots(iota(shape, 1), shards, ratio)
    return one_hot(used & (line == iota(shape, 0)))


def group_mask(shards, ratio, narrow, width):
    shape = (shards * SLOTS, width)
    _, group, used = packed_slots(iota(shape, 0), shards, ratio)
    column = iota(shape, 1) - group * narrow
    return used & (column >= 0) & (column < narrow)


def place_table(shards, narrow, width):
    lane = iota((width, LANES), 1)
    ahead = iota((width, LANES), 0) - lane
    found = ahead == 0
    for group in range(1, shards):
        found = found | (ahead == group * narrow)
    return one_hot(found & (lane < narrow))


def pack_local(local, narrow, ratio):
    vectors = [local[i].reshape(1, narrow) for i in NARROW] + [local[WIDE].reshape(ratio, narrow)]
    block = jnp.concatenate(vectors, axis=0)
    return jnp.pad(block, ((0, SLOTS - block.shape[0]), (0, LANES - narrow)))


def layer_kernel(shards, gather_cross, scatter_cross, *refs):
    chips, count = shards // 2, 7
    refs = list(refs)

    def take(number):
        taken = refs[:number]
        del refs[:number]
        return taken

    frames, cotangent = take(2)
    ins = take(count)
    result, d_start = take(2)
    outs = take(count)
    weights, terms, held, arrived, others = (take(count) for _ in range(5))
    found = take(sum(1 for cross in scatter_cross if cross))
    peers = [found.pop(0) if cross else None for cross in scatter_cross]
    (
        hat_one,
        inv_one,
        first,
        query,
        keys,
        values,
        probs,
        context,
        mixed,
        hat_two,
        inv_two,
        second,
        active,
        slope,
        d_inner,
        total,
        d_context,
        vec,
        gvec,
        place,
    ) = take(20)
    gather_sems, scatter_sems = take(7), take(8)
    frame_count, width = frames.shape
    hidden = slope.shape[1]
    ratio, narrow = hidden // width, width // shards
    ring = Ring(chips)
    gather = Gather(ring, chips, ins, weights, gather_cross, gather_sems)
    scatter = Scatter(
        ring, chips, terms, outs, held, arrived, peers, others, scatter_cross, scatter_sems
    )
    greet(ring, (ring.next(), ring.previous(), ring.mate), 2)

    early, late = (PACK, Q, K, V), (O, INNER)

    def hops(group, step):
        if 1 <= step < chips:
            for i in group:
                gather.hop(i, step)

    def crosses(group, step):
        if 1 <= step < chips:
            for i in group:
                gather.cross(i, step)

    def row(name):
        return vec[VECTOR[name] : VECTOR[name] + 1, :]

    def by_blocks(step):
        def go(block, carry):
            step(pl.ds(pl.multiple_of(block * BLOCK, BLOCK), BLOCK))
            return carry

        lax.fori_loop(0, frame_count // BLOCK, go, 0)

    def by_columns(start, stop, step, size=CHUNK):
        def go(chunk, carry):
            step(chunk)
            return carry

        lax.fori_loop(start, stop, go, 0)

    def columns(chunk, size=CHUNK):
        return pl.ds(pl.multiple_of(chunk * size, size), size)

    def add_row(index, value):
        gvec[index : index + 1, :] += value

    def sum_rows(value):
        return jnp.sum(value, axis=0, keepdims=True)

    for i in early:
        gather.start(i)
    for i in late:
        gather.start(i)

    gvec[...] = jnp.zeros_like(gvec)
    place[...] = place_table(shards, narrow, width)

    def start_norm(at):
        value = frames[at, :].astype(jnp.float32)
        centered = value - jnp.mean(value, axis=-1, keepdims=True)
        inv = lax.rsqrt(jnp.mean(centered * centered, axis=-1, keepdims=True) + EPSILON)
        inv_one[at, :] = inv
        hat_one[at, :] = centered * inv
        add_row(VECTOR[14], sum_rows(cotangent[at, :].astype(jnp.float32)))

    by_blocks(start_norm)

    for step in range(1, chips):
        hops(early, step)
        crosses(early, step - 1)
        hops(late, step - LAG)
        crosses(late, step - LAG - 1)
        if step == 4:
            gather.start(OUTER)
    crosses(early, chips - 1)
    for i in early:
        gather.finish(i)

    picks = pick_table(shards, ratio)
    spread = dot_nt(weights[PACK][...], place[...])
    spread = jnp.where(group_mask(shards, ratio, narrow, width), spread, 0.0)
    vec[...] = matmul(picks, spread.astype(jnp.bfloat16))

    queue = []

    def serve(number):
        for _ in range(min(number, len(queue))):
            queue.pop(0)()

    def later(call, *args):
        queue.append(functools.partial(call, *args))

    steps = range(1, chips)
    for step in range(chips - LAG, chips + 1):
        later(hops, late, step)
        later(crosses, late, step - 1)
    for step in range(1, chips + 1):
        later(hops, (OUTER,), step)
        later(crosses, (OUTER,), step - 1)

    def first_norm(at):
        value = hat_one[at, :] * row(0) + row(1)
        first[at, :] = value.astype(jnp.bfloat16)

    by_blocks(first_norm)

    def project(i, target, bias, scale):
        def go(chunk):
            at = columns(chunk)
            value = matmul(first[...], weights[i][:, at])
            if bias is not None:
                value = value + vec[VECTOR[bias] : VECTOR[bias] + 1, at]
            target[:, at] = (value * scale).astype(jnp.bfloat16)

        by_columns(0, width // CHUNK, go)

    project(Q, query, 3, HD ** (-0.5))
    serve(2)
    project(K, keys, None, 1.0)
    serve(2)
    project(V, values, 6, 1.0)
    serve(2)

    pair_width = 2 * HD
    pairs = width // pair_width
    lower = iota((1, pair_width), 1) < HD
    halves = (one_hot(lower), one_hot(jnp.logical_not(lower)))

    def attend(pair):
        at = pl.ds(pair * pair_width, pair_width)
        q_pair, k_pair, v_pair = query[:, at], keys[:, at], values[:, at]
        parts = []
        for half in range(2):
            scores = dot_nt(q_pair * halves[half], k_pair)
            grown = jnp.exp(scores - jnp.max(scores, axis=-1, keepdims=True))
            prob = (grown / jnp.sum(grown, axis=-1, keepdims=True)).astype(jnp.bfloat16)
            probs[2 * pair + half] = prob
            parts.append(matmul(prob, v_pair))
        context[:, at] = jnp.where(lower, parts[0], parts[1]).astype(jnp.bfloat16)

    for pair in range(pairs):
        attend(pair)
        serve(2)
    while len(queue) > 2 * chips:
        serve(1)

    for i in late:
        gather.finish(i)

    def mix(chunk):
        at = columns(chunk)
        value = matmul(context[...], weights[O][:, at])
        bias = vec[VECTOR[8] : VECTOR[8] + 1, at]
        mixed[:, at] = frames[:, at].astype(jnp.float32) + value + bias

    by_columns(0, width // CHUNK, mix)

    def second_norm(at):
        value = mixed[at, :]
        centered = value - jnp.mean(value, axis=-1, keepdims=True)
        inv = lax.rsqrt(jnp.mean(centered * centered, axis=-1, keepdims=True) + EPSILON)
        hat = centered * inv
        inv_two[at, :] = inv
        hat_two[at, :] = hat
        second[at, :] = (hat * row(9) + row(10)).astype(jnp.bfloat16)

    by_blocks(second_norm)
    serve(2)

    per_row = width // CHUNK

    def inner_step(line, chunk):
        inside = columns(chunk)
        at = columns(line * per_row + chunk)
        value = matmul(second[...], weights[INNER][:, at])
        value = value + vec[SPREAD + line : SPREAD + line + 1, inside]
        gelu, grad = gelu_parts(value)
        active[:, at] = gelu.astype(jnp.bfloat16)
        slope[:, at] = grad.astype(jnp.bfloat16)

    for line in range(ratio):
        by_columns(0, per_row, functools.partial(inner_step, line))
        serve(2)

    def outer_grad(chunk):
        at = columns(chunk)
        terms[OUTER][at, :] = dot_tn(active[:, at], cotangent[...]).astype(jnp.bfloat16)

    for line in range(ratio):
        by_columns(line * per_row, (line + 1) * per_row, outer_grad)
        serve(2)
    scatter.start(OUTER)
    serve(len(queue))
    gather.finish(OUTER)

    def plan(group):
        for i in group:
            later(scatter.give, i, 0)
        for step in range(chips):
            for i in group:
                if step + 1 < chips:
                    later(scatter.give, i, step + 1)
                later(scatter.hop, i, step)

    def inner_grad(line, chunk):
        inside = columns(chunk)
        at = columns(line * per_row + chunk)
        value = dot_nt(cotangent[...], weights[OUTER][at, :]) * slope[:, at].astype(jnp.float32)
        gvec[SPREAD + line : SPREAD + line + 1, inside] = sum_rows(value)
        low = value.astype(jnp.bfloat16)
        d_inner[:, at] = low
        terms[INNER][:, at] = dot_tn(second[...], low).astype(jnp.bfloat16)

    plan((OUTER,))
    for line in range(ratio):
        by_columns(0, per_row, functools.partial(inner_grad, line))
        serve(2)
    scatter.start(INNER)
    plan((INNER,))

    def second_back(chunk):
        at = columns(chunk)
        total[:, at] = dot_nt(d_inner[...], weights[INNER][at, :])

    by_columns(0, width // CHUNK, second_back)
    serve(2)

    def norm_step(grad_ref, hat_ref, inv_ref, gain, shift, at):
        grad, hat = grad_ref[at, :], hat_ref[at, :]
        add_row(VECTOR[gain], sum_rows(grad * hat))
        add_row(VECTOR[shift], sum_rows(grad))
        return norm_back(grad, hat, inv_ref[at, :], row(gain))

    def mixed_back(at):
        back = norm_step(total, hat_two, inv_two, 9, 10, at)
        value = cotangent[at, :].astype(jnp.float32) + back
        add_row(VECTOR[8], sum_rows(value))
        total[at, :] = value
        second[at, :] = value.astype(jnp.bfloat16)

    by_blocks(mixed_back)
    serve(2)

    def context_back(chunk):
        at = columns(chunk)
        d_context[:, at] = dot_nt(second[...], weights[O][at, :]).astype(jnp.bfloat16)

    by_columns(0, width // CHUNK, context_back)
    serve(2)

    def square_grad(i, left, right, chunk):
        at = columns(chunk)
        terms[i][at, :] = dot_tn(left[:, at], right[...]).astype(jnp.bfloat16)

    def grad_of(i, left, right):
        by_columns(0, width // CHUNK, functools.partial(square_grad, i, left, right))
        scatter.start(i)

    grad_of(O, context, second)
    plan((O,))
    serve(2)

    def attend_back(pair):
        at = pl.ds(pair * pair_width, pair_width)
        q_pair, k_pair, v_pair = query[:, at], keys[:, at], values[:, at]
        d_pair = d_context[:, at]
        product = d_pair.astype(jnp.float32) * context[:, at].astype(jnp.float32)
        d_q, d_k, d_v = [], [], []
        for half in range(2):
            prob = probs[2 * pair + half]
            inside = lower if half == 0 else jnp.logical_not(lower)
            delta = jnp.sum(jnp.where(inside, product, 0.0), axis=-1, keepdims=True)
            d_prob = dot_nt(d_pair * halves[half], v_pair)
            d_score = (prob.astype(jnp.float32) * (d_prob - delta)).astype(jnp.bfloat16)
            d_v.append(dot_tn(prob, d_pair))
            d_q.append(matmul(d_score, k_pair))
            d_k.append(dot_tn(d_score, q_pair))
        d_query = jnp.where(lower, d_q[0], d_q[1]) * HD ** (-0.5)
        d_values = jnp.where(lower, d_v[0], d_v[1])
        gvec[VECTOR[3] : VECTOR[3] + 1, at] = sum_rows(d_query)
        gvec[VECTOR[6] : VECTOR[6] + 1, at] = sum_rows(d_values)
        query[:, at] = d_query.astype(jnp.bfloat16)
        keys[:, at] = jnp.where(lower, d_k[0], d_k[1]).astype(jnp.bfloat16)
        values[:, at] = d_values.astype(jnp.bfloat16)

    for pair in range(pairs):
        attend_back(pair)
        serve(3)
    grad_of(V, first, values)
    serve(2)
    grad_of(K, first, keys)
    serve(2)
    grad_of(Q, first, query)
    serve(2)

    def first_back(chunk):
        at = columns(chunk)
        hat_two[:, at] = (
            dot_nt(query[...], weights[Q][at, :])
            + dot_nt(keys[...], weights[K][at, :])
            + dot_nt(values[...], weights[V][at, :])
        )

    by_columns(0, width // CHUNK, first_back)
    serve(2)

    def start_back(at):
        back = norm_step(hat_two, hat_one, inv_one, 0, 1, at)
        d_start[at, :] = (total[at, :] + back).astype(jnp.bfloat16)

    by_blocks(start_back)
    lines = dot_tn(picks, gvec[...].astype(jnp.bfloat16))
    lines = jnp.where(group_mask(shards, ratio, narrow, width), lines, 0.0)
    terms[PACK][...] = matmul(lines.astype(jnp.bfloat16), place[...]).astype(jnp.bfloat16)
    scatter.start(PACK)
    plan((V, K, Q, PACK))
    serve(8)

    def finish_result(chunk):
        at = columns(chunk)
        value = mixed[:, at] + matmul(active[...], weights[OUTER][:, at])
        bias = vec[VECTOR[14] : VECTOR[14] + 1, at]
        result[:, at] = (value + bias).astype(jnp.bfloat16)

    by_columns(0, width // CHUNK, finish_result)
    serve(len(queue))
    for i in (OUTER, INNER, O, V, K, Q, PACK):
        scatter.finish(i)
    for i in range(count):
        gather.drain(i)
        scatter.drain(i)


LAG = 2


def crossings(sizes, names, share):
    cut = [size // share for size in sizes]
    return tuple(c if i in names and c % SUBLANES == 0 else 0 for i, c in enumerate(cut))


def layer(frames, cotangent, pieces, shards):
    chips, (rows, width) = shards // 2, frames.shape
    hidden = pieces[INNER].shape[1]
    sizes = [piece.shape[0] for piece in pieces]
    wides = [piece.shape[1] for piece in pieces]
    gather_cross = crossings(sizes, range(6), 3)
    thirds = crossings(sizes, (V, O, INNER), 3)
    quarters = crossings(sizes, (OUTER,), 4)
    scatter_cross = tuple(a + b for a, b in zip(thirds, quarters))
    full = [(size * shards, wide) for size, wide in zip(sizes, wides)]
    ringed = [(size - cross, wide) for size, cross, wide in zip(sizes, scatter_cross, wides)]
    low, high = jnp.bfloat16, jnp.float32
    dma = pltpu.SemaphoreType.DMA
    scratch = (
        [pltpu.VMEM(shape, low) for shape in full] * 2
        + [pltpu.VMEM((chips, size, wide), low) for size, wide in zip(sizes, wides)]
        + [pltpu.VMEM((chips - 1,) + shape, low) for shape in ringed]
        + [pltpu.VMEM(shape, low) for shape in ringed]
        + [
            pltpu.VMEM((chips, cross, wide), low)
            for cross, wide in zip(scatter_cross, wides)
            if cross
        ]
        + [
            pltpu.VMEM((rows, width), high),
            pltpu.VMEM((rows, 1), high),
            pltpu.VMEM((rows, width), low),
            pltpu.VMEM((rows, width), low),
            pltpu.VMEM((rows, width), low),
            pltpu.VMEM((rows, width), low),
            pltpu.VMEM((width // HD, rows, rows), low),
            pltpu.VMEM((rows, width), low),
            pltpu.VMEM((rows, width), high),
            pltpu.VMEM((rows, width), high),
            pltpu.VMEM((rows, 1), high),
            pltpu.VMEM((rows, width), low),
            pltpu.VMEM((rows, hidden), low),
            pltpu.VMEM((rows, hidden), low),
            pltpu.VMEM((rows, hidden), low),
            pltpu.VMEM((rows, width), high),
            pltpu.VMEM((rows, width), low),
            pltpu.VMEM((SLOTS, width), high),
            pltpu.VMEM((SLOTS, width), high),
            pltpu.VMEM((width, LANES), low),
        ]
        + [dma((chips, 7))] * 6
        + [dma((7,))]
        + [dma((chips, 7))] * 6
        + [dma((7,))] * 2
    )
    vmem = pl.BlockSpec(memory_space=pltpu.VMEM)
    return pl.pallas_call(
        functools.partial(layer_kernel, shards, gather_cross, scatter_cross),
        out_shape=[jax.ShapeDtypeStruct((rows, width), low)] * 2
        + [jax.ShapeDtypeStruct(shape, high) for shape in zip(sizes, wides)],
        in_specs=[vmem] * 2 + [pl.BlockSpec(memory_space=pl.ANY)] * 7,
        out_specs=[vmem] * 9,
        scratch_shapes=scratch,
        compiler_params=pltpu.CompilerParams(
            collective_id=2, has_side_effects=True, vmem_limit_bytes=67043328
        ),
        name="layer",
    )(frames, cotangent, *pieces)


def fits(shards, reps, frames, local):
    narrow, wide = local[0].shape[0], local[WIDE].shape[0]
    return (
        reps == 2
        and shards >= 4
        and shards & (shards - 1) == 0
        and frames.shape[0] == 1
        and frames.shape[1] % CHUNK == 0
        and frames.shape[2] % CHUNK == 0
        and all(local[i].shape[0] % (3 * SUBLANES) == 0 for i in WEIGHTS)
        and wide % narrow == 0
        and SPREAD + wide // narrow <= SLOTS
        and narrow <= LANES
    )


def per_device(shards, reps, frames, cotangent, *local):
    if not fits(shards, reps, frames, local):
        return per_device_plain(shards, reps, frames, cotangent, *local)
    narrow, wide = local[0].shape[0], local[WIDE].shape[0]
    ratio = wide // narrow
    pieces = [local[i] for i in WEIGHTS] + [pack_local(local, narrow, ratio)]
    result, d_start, *sums = layer(frames[0], cotangent[0], pieces, shards)
    out = [None] * len(local)
    for k, i in enumerate(WEIGHTS):
        out[i] = sums[k]
    for k, i in enumerate(NARROW):
        out[i] = sums[PACK][k, :narrow]
    out[WIDE] = sums[PACK][SPREAD : SPREAD + ratio, :narrow].reshape(-1)
    return (result[None], d_start[None], *out)


def solution(mesh):
    clips = P(("shard", "rep"), None, None)
    weights = tuple(P("shard", None) if i in WEIGHTS else P("shard") for i in range(15))
    return jax.shard_map(
        functools.partial(per_device, mesh.shape["shard"], mesh.shape["rep"]),
        mesh=mesh,
        in_specs=(clips, clips) + weights,
        out_specs=(clips, clips) + weights,
        check_vma=False,
    )
```

```python
import functools

import jax
import jax.numpy as jnp
from jax import lax
from jax.experimental import pallas as pl
from jax.experimental.pallas import tpu as pltpu
from jax.sharding import PartitionSpec as P

D = 768
HEADS = 12
HD = 64


EPSILON = 1e-05


def normalize(values, gain, shift):
    center = jnp.mean(values, axis=-1, keepdims=True)
    spread = jnp.mean((values - center) ** 2, axis=-1, keepdims=True)
    inv_std = lax.rsqrt(spread + EPSILON)
    normed = (values - center) * inv_std
    return (normed * gain.astype(jnp.float32) + shift.astype(jnp.float32), normed, inv_std)


def norm_back(grad_out, normed, inv_std, gain):
    scaled = grad_out * gain.astype(jnp.float32)
    return inv_std * (
        scaled
        - jnp.mean(scaled, axis=-1, keepdims=True)
        - normed * jnp.mean(scaled * normed, axis=-1, keepdims=True)
    )


def gelu_parts(inner):
    cdf = 0.5 * (1.0 + jax.scipy.special.erf(inner * 0.7071067811865476))
    density = jnp.exp(-0.5 * inner * inner) * 0.3989422804014327
    return (inner * cdf, cdf + inner * density)


def heads_of(matrix):
    return matrix.reshape(matrix.shape[0], HEADS, HD)


def matmul(left, right):
    return jnp.dot(left, right, preferred_element_type=jnp.float32)


def forward_clip(clip, params):
    (
        first_gain,
        first_shift,
        query_weight,
        query_bias,
        key_weight,
        value_weight,
        value_bias,
        output_weight,
        output_bias,
        second_gain,
        second_shift,
        inner_weight,
        inner_bias,
        outer_weight,
        outer_bias,
    ) = params
    start = clip.astype(jnp.float32)
    normed_one, hat_one, inv_one = normalize(start, first_gain, first_shift)
    first_low = normed_one.astype(jnp.bfloat16)
    query = (
        (matmul(first_low, query_weight) + query_bias.astype(jnp.float32)) * HD ** (-0.5)
    ).astype(jnp.bfloat16)
    keys = matmul(first_low, key_weight).astype(jnp.bfloat16)
    values = (matmul(first_low, value_weight) + value_bias.astype(jnp.float32)).astype(jnp.bfloat16)
    scores = jnp.einsum(
        "qhd,khd->hqk", heads_of(query), heads_of(keys), preferred_element_type=jnp.float32
    )
    highest = jnp.max(scores, axis=-1, keepdims=True)
    log_total = highest + jnp.log(jnp.sum(jnp.exp(scores - highest), axis=-1, keepdims=True))
    probs = jnp.exp(scores - log_total).astype(jnp.bfloat16)
    context = (
        jnp.einsum("hqk,khd->qhd", probs, heads_of(values), preferred_element_type=jnp.float32)
        .reshape(-1, D)
        .astype(jnp.bfloat16)
    )
    mixed = start + matmul(context, output_weight) + output_bias.astype(jnp.float32)
    normed_two, hat_two, inv_two = normalize(mixed, second_gain, second_shift)
    second_low = normed_two.astype(jnp.bfloat16)
    inner = matmul(second_low, inner_weight) + inner_bias.astype(jnp.float32)
    active, slope = gelu_parts(inner)
    active_low = active.astype(jnp.bfloat16)
    result = (mixed + matmul(active_low, outer_weight) + outer_bias.astype(jnp.float32)).astype(
        jnp.bfloat16
    )
    saved = (
        hat_one,
        inv_one,
        first_low,
        query,
        keys,
        values,
        log_total,
        context,
        hat_two,
        inv_two,
        second_low,
        slope,
        active_low,
    )
    return (result, saved)


def backward_clip(grad_low, saved, params):
    (
        first_gain,
        first_shift,
        query_weight,
        query_bias,
        key_weight,
        value_weight,
        value_bias,
        output_weight,
        output_bias,
        second_gain,
        second_shift,
        inner_weight,
        inner_bias,
        outer_weight,
        outer_bias,
    ) = params
    (
        hat_one,
        inv_one,
        first_low,
        query,
        keys,
        values,
        log_total,
        context,
        hat_two,
        inv_two,
        second_low,
        slope,
        active_low,
    ) = saved
    grad = grad_low.astype(jnp.float32)
    g_outer_bias = jnp.sum(grad, axis=0)
    g_outer = matmul(active_low.T, grad_low)
    d_inner = matmul(grad_low, outer_weight.T) * slope
    d_inner_low = d_inner.astype(jnp.bfloat16)
    g_inner_bias = jnp.sum(d_inner, axis=0)
    g_inner = matmul(second_low.T, d_inner_low)
    d_second = matmul(d_inner_low, inner_weight.T)
    g_second_gain = jnp.sum(d_second * hat_two, axis=0)
    g_second_shift = jnp.sum(d_second, axis=0)
    d_mixed = grad + norm_back(d_second, hat_two, inv_two, second_gain)
    d_mixed_low = d_mixed.astype(jnp.bfloat16)
    g_output_bias = jnp.sum(d_mixed, axis=0)
    g_output = matmul(context.T, d_mixed_low)
    d_context = matmul(d_mixed_low, output_weight.T).astype(jnp.bfloat16)
    query_heads = heads_of(query)
    keys_heads = heads_of(keys)
    values_heads = heads_of(values)
    dctx_heads = heads_of(d_context)
    scores = jnp.einsum("qhd,khd->hqk", query_heads, keys_heads, preferred_element_type=jnp.float32)
    probs = jnp.exp(scores - log_total)
    probs_low = probs.astype(jnp.bfloat16)
    d_probs = jnp.einsum(
        "qhd,khd->hqk", dctx_heads, values_heads, preferred_element_type=jnp.float32
    )
    delta = jnp.sum(dctx_heads.astype(jnp.float32) * heads_of(context).astype(jnp.float32), axis=-1)
    d_scores = (probs * (d_probs - jnp.transpose(delta)[:, :, None])).astype(jnp.bfloat16)
    d_values = jnp.einsum(
        "hqk,qhd->khd", probs_low, dctx_heads, preferred_element_type=jnp.float32
    ).reshape(-1, D)
    d_query = jnp.einsum(
        "hqk,khd->qhd", d_scores, keys_heads, preferred_element_type=jnp.float32
    ).reshape(-1, D) * HD ** (-0.5)
    d_keys = jnp.einsum(
        "hqk,qhd->khd", d_scores, query_heads, preferred_element_type=jnp.float32
    ).reshape(-1, D)
    dq_low = d_query.astype(jnp.bfloat16)
    dk_low = d_keys.astype(jnp.bfloat16)
    dv_low = d_values.astype(jnp.bfloat16)
    g_query_bias = jnp.sum(d_query, axis=0)
    g_value_bias = jnp.sum(d_values, axis=0)
    g_query = matmul(first_low.T, dq_low)
    g_keys = matmul(first_low.T, dk_low)
    g_values = matmul(first_low.T, dv_low)
    d_first = (
        matmul(dq_low, query_weight.T)
        + matmul(dk_low, key_weight.T)
        + matmul(dv_low, value_weight.T)
    )
    g_first_gain = jnp.sum(d_first * hat_one, axis=0)
    g_first_shift = jnp.sum(d_first, axis=0)
    d_start = (d_mixed + norm_back(d_first, hat_one, inv_one, first_gain)).astype(jnp.bfloat16)
    grads = (
        g_first_gain,
        g_first_shift,
        g_query,
        g_query_bias,
        g_keys,
        g_values,
        g_value_bias,
        g_output,
        g_output_bias,
        g_second_gain,
        g_second_shift,
        g_inner,
        g_inner_bias,
        g_outer,
        g_outer_bias,
    )
    return (d_start, grads)


MESH = pl.DeviceIdType.MESH


class Ring:
    def __init__(self, chips):
        self.chips = chips
        shard = lax.axis_index("shard")
        self.rep = lax.axis_index("rep")
        self.core = lax.rem(shard, 2)
        chip = shard // 2
        half = chip // 2
        self.pos = half + lax.rem(chip, 2) * (chips - 1 - 2 * half)
        self.step = 1 - 2 * self.core
        self.me = shard
        self.mate = chip * 2 + (1 - self.core)

    def shard_at(self, offset, core):
        place = lax.rem(self.pos + offset + 2 * self.chips, self.chips)
        far = place // (self.chips // 2)
        chip = (1 - far) * 2 * place + far * (2 * (self.chips - 1 - place) + 1)
        return chip * 2 + core

    def next(self):
        return self.shard_at(self.step, self.core)

    def previous(self):
        return self.shard_at(-self.step, self.core)


def rows_of(owner, rows):
    return pl.ds(pl.multiple_of(owner * rows, rows), rows)


def greet(ring, others, reps):
    barrier = pltpu.get_barrier_semaphore()
    for other in others:
        pl.semaphore_signal(barrier, inc=1, device_id=(other, ring.rep), device_id_type=MESH)
    for shift in range(1, reps):
        pl.semaphore_signal(
            barrier,
            inc=1,
            device_id=(ring.me, lax.rem(ring.rep + shift, reps)),
            device_id_type=MESH,
        )
    pl.semaphore_wait(barrier, len(others) + reps - 1)


def gather_kernel(chips, count, *refs):
    ins, outs = refs[:count], refs[count : 2 * count]
    ring_send, ring_recv, mate_send, mate_recv, own_sem = refs[2 * count :]
    ring = Ring(chips)
    core = ring.core
    following, mate = ring.next(), ring.mate
    greet(ring, (following, ring.previous(), mate), 1)

    def where(index, owner):
        return outs[index].at[rows_of(owner, ins[index].shape[0])]

    def to_next(index, step, owner, source):
        return pltpu.make_async_remote_copy(
            src_ref=source,
            dst_ref=where(index, owner),
            send_sem=ring_send.at[step, index],
            recv_sem=ring_recv.at[step, index],
            device_id=(following, ring.rep),
            device_id_type=MESH,
        )

    def to_mate(index, step, owner, source):
        return pltpu.make_async_remote_copy(
            src_ref=source,
            dst_ref=where(index, owner),
            send_sem=mate_send.at[step, index],
            recv_sem=mate_recv.at[step, index],
            device_id=(mate, ring.rep),
            device_id_type=MESH,
        )

    for index in range(count):
        to_next(index, 0, ring.me, ins[index]).start()
    for index in range(count):
        to_mate(index, 0, ring.me, ins[index]).start()
        pltpu.make_async_copy(ins[index], where(index, ring.me), own_sem.at[index]).start()

    def hop(step, carry):
        owner = ring.shard_at(-ring.step * step, core)
        for index in range(count):
            block = where(index, owner)
            to_next(index, step - 1, owner, block).wait_recv()
            pl.when(step < chips - 1)(lambda: to_next(index, step, owner, block).start())
            to_mate(index, step, owner, block).start()
        return carry

    lax.fori_loop(1, chips, hop, 0)

    def finish(step, carry):
        owner = ring.shard_at(-ring.step * step, core)
        theirs = ring.shard_at(ring.step * step, 1 - core)
        for index in range(count):
            to_mate(index, step, theirs, where(index, theirs)).wait_recv()
            to_mate(index, step, owner, where(index, owner)).wait_send()
            pl.when(step < chips - 1)(
                lambda: to_next(index, step, owner, where(index, owner)).wait_send()
            )
        return carry

    lax.fori_loop(0, chips, finish, 0)
    for index in range(count):
        pltpu.make_async_copy(ins[index], where(index, ring.me), own_sem.at[index]).wait()


def gather_all(pieces, shards):
    chips, count = shards // 2, len(pieces)
    return pl.pallas_call(
        functools.partial(gather_kernel, chips, count),
        out_shape=[
            jax.ShapeDtypeStruct((piece.shape[0] * shards, piece.shape[1]), piece.dtype)
            for piece in pieces
        ],
        in_specs=[pl.BlockSpec(memory_space=pltpu.VMEM)] * count,
        out_specs=[pl.BlockSpec(memory_space=pl.ANY)] * count,
        scratch_shapes=[
            pltpu.SemaphoreType.DMA((chips, count)),
            pltpu.SemaphoreType.DMA((chips, count)),
            pltpu.SemaphoreType.DMA((chips, count)),
            pltpu.SemaphoreType.DMA((chips, count)),
            pltpu.SemaphoreType.DMA((count,)),
        ],
        compiler_params=pltpu.CompilerParams(collective_id=0, has_side_effects=True),
        name="gather_all",
    )(*pieces)


def scatter_kernel(chips, reps, count, *refs):
    ins, outs = refs[:count], refs[count : 2 * count]
    held = refs[2 * count : 3 * count]
    arrived = refs[3 * count : 4 * count]
    peers = refs[4 * count : 5 * count]
    ring_send, ring_recv, mate_send, mate_recv, rep_send, rep_recv = refs[5 * count :]
    ring = Ring(chips)
    core = ring.core
    following, mate = ring.next(), ring.mate
    greet(ring, (following, ring.previous(), mate), reps)

    def to_mate(index, step):
        owner = ring.shard_at(ring.step * (step + 1), 1 - core)
        rows = outs[index].shape[0]
        return pltpu.make_async_remote_copy(
            src_ref=ins[index].at[rows_of(owner, rows)],
            dst_ref=held[index].at[step],
            send_sem=mate_send.at[step, index],
            recv_sem=mate_recv.at[step, index],
            device_id=(mate, ring.rep),
            device_id_type=MESH,
        )

    def to_next(index, step):
        return pltpu.make_async_remote_copy(
            src_ref=held[index].at[step],
            dst_ref=arrived[index].at[step],
            send_sem=ring_send.at[step, index],
            recv_sem=ring_recv.at[step, index],
            device_id=(following, ring.rep),
            device_id_type=MESH,
        )

    def to_rep(index, shift):
        return pltpu.make_async_remote_copy(
            src_ref=held[index].at[chips - 1],
            dst_ref=peers[index].at[ring.rep],
            send_sem=rep_send.at[shift, index],
            recv_sem=rep_recv.at[shift, index],
            device_id=(ring.me, lax.rem(ring.rep + shift, reps)),
            device_id_type=MESH,
        )

    def hand_over(step, carry):
        for index in range(count):
            to_mate(index, step).start()
        return carry

    lax.fori_loop(0, chips, hand_over, 0)

    def add(index, step, first):
        owner = ring.shard_at(-ring.step * (step + 1), core)
        rows = outs[index].shape[0]
        to_mate(index, step).wait_recv()
        total = ins[index][rows_of(owner, rows), :].astype(jnp.float32) + held[index][step].astype(
            jnp.float32
        )
        if not first:
            to_next(index, step - 1).wait_recv()
            total = total + arrived[index][step - 1].astype(jnp.float32)
        held[index][step] = total.astype(jnp.bfloat16)

    for index in range(count):
        add(index, 0, True)
        to_next(index, 0).start()

    def hop(step, carry):
        for index in range(count):
            add(index, step, False)
            to_next(index, step).start()
        return carry

    lax.fori_loop(1, chips - 1, hop, 0)
    for index in range(count):
        add(index, chips - 1, False)
        for shift in range(1, reps):
            to_rep(index, shift).start()
        peers[index][ring.rep] = held[index][chips - 1]
    for index in range(count):
        for shift in range(1, reps):
            to_rep(index, shift).wait_recv()
        total = peers[index][0].astype(jnp.float32)
        for rep in range(1, reps):
            total = total + peers[index][rep].astype(jnp.float32)
        outs[index][...] = total

    def finish(step, carry):
        for index in range(count):
            to_mate(index, step).wait_send()
            pl.when(step < chips - 1)(lambda: to_next(index, step).wait_send())
        return carry

    lax.fori_loop(0, chips, finish, 0)
    for index in range(count):
        for shift in range(1, reps):
            to_rep(index, shift).wait_send()


def scatter_all(pieces, shards, reps):
    chips, count = shards // 2, len(pieces)
    blocks = [(piece.shape[0] // shards, piece.shape[1]) for piece in pieces]
    return pl.pallas_call(
        functools.partial(scatter_kernel, chips, reps, count),
        out_shape=[jax.ShapeDtypeStruct(block, jnp.float32) for block in blocks],
        in_specs=[pl.BlockSpec(memory_space=pltpu.VMEM)] * count,
        out_specs=[pl.BlockSpec(memory_space=pltpu.VMEM)] * count,
        scratch_shapes=[pltpu.VMEM((chips,) + block, jnp.bfloat16) for block in blocks]
        + [pltpu.VMEM((chips - 1,) + block, jnp.bfloat16) for block in blocks]
        + [pltpu.VMEM((reps,) + block, jnp.bfloat16) for block in blocks]
        + [pltpu.SemaphoreType.DMA((chips, count))] * 4
        + [pltpu.SemaphoreType.DMA((reps, count))] * 2,
        compiler_params=pltpu.CompilerParams(
            collective_id=1, has_side_effects=True, vmem_limit_bytes=60 * 1024 * 1024
        ),
        name="scatter_all",
    )(*pieces)


NARROW = (0, 1, 3, 6, 8, 9, 10, 14)
WIDE = 12
WEIGHTS = (2, 4, 5, 7, 11, 13)
LANES = 128
SUBLANES = 16


def packed_rows(size):
    return -(-size // (LANES * SUBLANES)) * SUBLANES


def pack(vectors, owners):
    flat = jnp.concatenate(
        [vectors[i].reshape(owners, -1) for i in NARROW] + [vectors[WIDE].reshape(owners, -1)],
        axis=1,
    )
    rows = packed_rows(flat.shape[1])
    flat = jnp.pad(flat, ((0, 0), (0, rows * LANES - flat.shape[1])))
    return flat.reshape(owners * rows, LANES)


def unpack(block, owners, narrow, wide):
    flat = block.reshape(owners, -1)
    count = len(NARROW)
    first = flat[:, : count * narrow].reshape(owners, count, narrow)
    first = jnp.transpose(first, (1, 0, 2)).reshape(count, owners * narrow)
    found = {i: first[k] for k, i in enumerate(NARROW)}
    found[WIDE] = flat[:, count * narrow : count * narrow + wide].reshape(-1)
    return found


def per_device_plain(shards, reps, frames, cotangent, *local):
    narrow, wide = local[0].shape[0], local[WIDE].shape[0]
    gathered = gather_all([local[i] for i in WEIGHTS] + [pack(local, 1)], shards)
    params = [None] * len(local)
    for k, i in enumerate(WEIGHTS):
        params[i] = gathered[k]
    for i, vector in unpack(gathered[-1], shards, narrow, wide).items():
        params[i] = vector
    params = tuple(params)

    results, input_grads, totals = [], [], None
    for k in range(frames.shape[0]):
        result, saved = forward_clip(frames[k], params)
        d_start, grads = backward_clip(cotangent[k], saved, params)
        results.append(result)
        input_grads.append(d_start)
        totals = grads if totals is None else tuple(a + b for a, b in zip(totals, grads))

    low = [total.astype(jnp.bfloat16) for total in totals]
    summed = scatter_all([low[i] for i in WEIGHTS] + [pack(low, shards)], shards, reps)
    out = [None] * len(local)
    for k, i in enumerate(WEIGHTS):
        out[i] = summed[k]
    for i, vector in unpack(summed[-1], 1, narrow, wide).items():
        out[i] = vector
    return (jnp.stack(results), jnp.stack(input_grads), *out)


TN = (((0,), (0,)), ((), ()))
NT = (((1,), (1,)), ((), ()))
CHUNK = 256
BLOCK = 32


def dot_tn(left, right):
    return lax.dot_general(left, right, TN, preferred_element_type=jnp.float32)


def dot_nt(left, right):
    return lax.dot_general(left, right, NT, preferred_element_type=jnp.float32)


def span(start, size, unit):
    return pl.ds(pl.multiple_of(start, unit), size)


class Gather:
    def __init__(self, ring, chips, ins, outs, crossed, sems):
        self.ring, self.chips, self.ins, self.outs, self.crossed = ring, chips, ins, outs, crossed
        (
            self.ring_send,
            self.ring_recv,
            self.mate_send,
            self.mate_recv,
            self.peer_send,
            self.peer_recv,
            self.own_sem,
        ) = sems
        self.next, self.mate = ring.next(), ring.mate

    def rows(self, i):
        return self.ins[i].shape[0]

    def part(self, i, kind):
        rows, cross = self.rows(i), self.crossed[i]
        if kind == "all":
            return 0, rows
        if kind == "ringed":
            return self.ring.rep * cross, rows - cross
        if kind == "sent":
            return self.ring.rep * (rows - cross), cross
        return (1 - self.ring.rep) * (rows - cross), cross

    def remote(self, i, step, owner, kind, send, recv, target, own=False):
        offset, size = self.part(i, kind)
        place = self.outs[i].at[span(owner * self.rows(i) + offset, size, SUBLANES)]
        source = self.ins[i].at[span(offset, size, SUBLANES)] if own else place
        return pltpu.make_async_remote_copy(
            src_ref=source,
            dst_ref=place,
            send_sem=send.at[step, i],
            recv_sem=recv.at[step, i],
            device_id=target,
            device_id_type=MESH,
        )

    def to_next(self, i, step, owner, own=False):
        target = (self.next, self.ring.rep)
        return self.remote(
            i, step, owner, "ringed", self.ring_send, self.ring_recv, target, own
        )

    def to_mate(self, i, step, owner, kind, own=False):
        target = (self.mate, self.ring.rep)
        return self.remote(i, step, owner, kind, self.mate_send, self.mate_recv, target, own)

    def to_peer(self, i, step, owner, kind):
        target = (self.ring.me, 1 - self.ring.rep)
        return self.remote(i, step, owner, kind, self.peer_send, self.peer_recv, target)

    def own_copy(self, i):
        place = self.outs[i].at[span(self.ring.me * self.rows(i), self.rows(i), SUBLANES)]
        return pltpu.make_async_copy(self.ins[i], place, self.own_sem.at[i])

    def owner(self, step):
        return self.ring.shard_at(-self.ring.step * step, self.ring.core)

    def start(self, i):
        self.to_next(i, 0, self.ring.me, True).start()
        self.to_mate(i, 0, self.ring.me, "all", True).start()
        self.own_copy(i).start()

    def hop(self, i, step):
        owner = self.owner(step)
        self.to_next(i, step - 1, owner).wait_recv()
        if step < self.chips - 1:
            self.to_next(i, step, owner).start()
        if self.crossed[i]:
            self.to_peer(i, step, owner, "sent").start()
        self.to_mate(i, step, owner, "ringed").start()

    def cross(self, i, step):
        if self.crossed[i]:
            owner = self.owner(step)
            self.to_peer(i, step, owner, "got").wait_recv()
            self.to_mate(i, step, owner, "got").start()

    def finish(self, i):
        for step in range(self.chips):
            theirs = self.ring.shard_at(self.ring.step * step, 1 - self.ring.core)
            self.to_mate(i, step, theirs, "all").wait_recv()
        self.own_copy(i).wait()

    def drain(self, i):
        for step in range(self.chips):
            owner = self.owner(step)
            self.to_mate(i, step, owner, "all").wait_send()
            if step < self.chips - 1:
                self.to_next(i, step, owner).wait_send()
            if step and self.crossed[i]:
                self.to_peer(i, step, owner, "sent").wait_send()


class Scatter:
    def __init__(self, ring, chips, terms, outs, held, arrived, peers, others, crossed, sems):
        self.ring, self.chips, self.terms, self.outs = ring, chips, terms, outs
        self.held, self.arrived, self.peers, self.others = held, arrived, peers, others
        self.crossed = crossed
        (
            self.mate_send,
            self.mate_recv,
            self.ring_send,
            self.ring_recv,
            self.peer_send,
            self.peer_recv,
            self.last_send,
            self.last_recv,
        ) = sems
        self.next, self.mate = ring.next(), ring.mate

    def rows(self, i):
        return self.outs[i].shape[0]

    def spots(self, i):
        rep, rows, cross = self.ring.rep, self.rows(i), self.crossed[i]
        return {
            "ringed": rep * cross,
            "kept": rep * (rows - cross),
            "middle": cross,
            "given": (1 - rep) * (rows - cross),
            "kept_in": rep * (rows - 2 * cross),
            "middle_in": (1 - rep) * cross,
            "other_kept_in": (1 - rep) * (rows - 2 * cross),
            "other_middle_in": rep * cross,
        }

    def copy(self, source, target, send, recv, device):
        return pltpu.make_async_remote_copy(
            src_ref=source,
            dst_ref=target,
            send_sem=send,
            recv_sem=recv,
            device_id=device,
            device_id_type=MESH,
        )

    def owner(self, step):
        return self.ring.shard_at(-self.ring.step * (step + 1), self.ring.core)

    def to_mate(self, i, step):
        owner = self.ring.shard_at(self.ring.step * (step + 1), 1 - self.ring.core)
        return self.copy(
            self.terms[i].at[rows_of(owner, self.rows(i))],
            self.held[i].at[step],
            self.mate_send.at[step, i],
            self.mate_recv.at[step, i],
            (self.mate, self.ring.rep),
        )

    def to_next(self, i, step):
        size = self.rows(i) - self.crossed[i]
        return self.copy(
            self.held[i].at[step, span(self.spots(i)["ringed"], size, SUBLANES)],
            self.arrived[i].at[step],
            self.ring_send.at[step, i],
            self.ring_recv.at[step, i],
            (self.next, self.ring.rep),
        )

    def to_peer(self, i, step):
        return self.copy(
            self.held[i].at[step, span(self.spots(i)["given"], self.crossed[i], SUBLANES)],
            self.peers[i].at[step],
            self.peer_send.at[step, i],
            self.peer_recv.at[step, i],
            (self.ring.me, 1 - self.ring.rep),
        )

    def to_last(self, i):
        size = self.rows(i) - self.crossed[i]
        return self.copy(
            self.held[i].at[self.chips - 1, span(self.spots(i)["ringed"], size, SUBLANES)],
            self.others[i],
            self.last_send.at[i],
            self.last_recv.at[i],
            (self.ring.me, 1 - self.ring.rep),
        )

    def start(self, i):
        for step in range(self.chips):
            self.to_mate(i, step).start()

    def both(self, i, step, offset, size):
        mine = self.terms[i][span(self.owner(step) * self.rows(i) + offset, size, SUBLANES), :]
        theirs = self.held[i][step, span(offset, size, SUBLANES), :]
        return mine.astype(jnp.float32) + theirs.astype(jnp.float32)

    def keep(self, i, step, offset, total):
        place = span(offset, total.shape[0], SUBLANES)
        self.held[i][step, place, :] = total.astype(jnp.bfloat16)

    def give(self, i, step):
        self.to_mate(i, step).wait_recv()
        if self.crossed[i]:
            offset = self.spots(i)["given"]
            self.keep(i, step, offset, self.both(i, step, offset, self.crossed[i]))
            self.to_peer(i, step).start()

    def hop(self, i, step):
        spots, cross = self.spots(i), self.crossed[i]
        middle = self.rows(i) - 2 * cross
        if step:
            self.to_next(i, step - 1).wait_recv()
        total = self.both(i, step, spots["middle"], middle)
        if step:
            part = self.arrived[i][step - 1, span(spots["middle_in"], middle, SUBLANES), :]
            total = total + part.astype(jnp.float32)
        self.keep(i, step, spots["middle"], total)
        if cross:
            self.to_peer(i, step).wait_recv()
            total = self.both(i, step, spots["kept"], cross)
            total = total + self.peers[i][step].astype(jnp.float32)
            if step:
                part = self.arrived[i][step - 1, span(spots["kept_in"], cross, SUBLANES), :]
                total = total + part.astype(jnp.float32)
            self.keep(i, step, spots["kept"], total)
        if step < self.chips - 1:
            self.to_next(i, step).start()
        else:
            self.to_last(i).start()

    def finish(self, i):
        spots, cross = self.spots(i), self.crossed[i]
        middle, last = self.rows(i) - 2 * cross, self.chips - 1
        self.to_last(i).wait_recv()
        mine = self.held[i][last, span(spots["middle"], middle, SUBLANES), :]
        theirs = self.others[i][span(spots["other_middle_in"], middle, SUBLANES), :]
        self.outs[i][span(spots["middle"], middle, SUBLANES), :] = mine.astype(
            jnp.float32
        ) + theirs.astype(jnp.float32)
        if cross:
            kept = span(spots["kept"], cross, SUBLANES)
            self.outs[i][kept, :] = self.held[i][last, kept, :].astype(jnp.float32)
            other = self.others[i][span(spots["other_kept_in"], cross, SUBLANES), :]
            given = span(spots["given"], cross, SUBLANES)
            self.outs[i][given, :] = other.astype(jnp.float32)

    def drain(self, i):
        for step in range(self.chips):
            self.to_mate(i, step).wait_send()
            if step < self.chips - 1:
                self.to_next(i, step).wait_send()
            if self.crossed[i]:
                self.to_peer(i, step).wait_send()
        self.to_last(i).wait_send()


Q, K, V, O, INNER, OUTER, PACK = range(7)
SLOTS = 16
SPREAD = len(NARROW)
VECTOR = {name: row for row, name in enumerate(NARROW)}


def iota(shape, axis):
    return lax.broadcasted_iota(jnp.int32, shape, axis)


def one_hot(condition):
    return jnp.where(condition, 1.0, 0.0).astype(jnp.bfloat16)


def bits(size):
    return size.bit_length() - 1


def packed_slots(index, shards, ratio):
    owner, slot = index >> bits(SLOTS), index & (SLOTS - 1)
    wide = owner * ratio + slot - SPREAD
    line = jnp.where(slot < SPREAD, slot, SPREAD + (wide >> bits(shards)))
    group = jnp.where(slot < SPREAD, owner, wide & (shards - 1))
    return line, group, slot < SPREAD + ratio


def pick_table(shards, ratio):
    shape = (SLOTS, shards * SLOTS)
    line, _, used = packed_slots(iota(shape, 1), shards, ratio)
    return one_hot(used & (line == iota(shape, 0)))


def group_mask(shards, ratio, narrow, width):
    shape = (shards * SLOTS, width)
    _, group, used = packed_slots(iota(shape, 0), shards, ratio)
    column = iota(shape, 1) - group * narrow
    return used & (column >= 0) & (column < narrow)


def place_table(shards, narrow, width):
    lane = iota((width, LANES), 1)
    ahead = iota((width, LANES), 0) - lane
    found = ahead == 0
    for group in range(1, shards):
        found = found | (ahead == group * narrow)
    return one_hot(found & (lane < narrow))


def pack_local(local, narrow, ratio):
    vectors = [local[i].reshape(1, narrow) for i in NARROW] + [local[WIDE].reshape(ratio, narrow)]
    block = jnp.concatenate(vectors, axis=0)
    return jnp.pad(block, ((0, SLOTS - block.shape[0]), (0, LANES - narrow)))


def layer_kernel(shards, gather_cross, scatter_cross, *refs):
    chips, count = shards // 2, 7
    refs = list(refs)

    def take(number):
        taken = refs[:number]
        del refs[:number]
        return taken

    frames, cotangent = take(2)
    ins = take(count)
    result, d_start = take(2)
    outs = take(count)
    weights, terms, held, arrived, others = (take(count) for _ in range(5))
    found = take(sum(1 for cross in scatter_cross if cross))
    peers = [found.pop(0) if cross else None for cross in scatter_cross]
    (
        hat_one,
        inv_one,
        first,
        query,
        keys,
        values,
        probs,
        context,
        mixed,
        hat_two,
        inv_two,
        second,
        active,
        slope,
        d_inner,
        total,
        d_context,
        vec,
        gvec,
        place,
    ) = take(20)
    gather_sems, scatter_sems = take(7), take(8)
    frame_count, width = frames.shape
    hidden = slope.shape[1]
    ratio, narrow = hidden // width, width // shards
    ring = Ring(chips)
    gather = Gather(ring, chips, ins, weights, gather_cross, gather_sems)
    scatter = Scatter(
        ring, chips, terms, outs, held, arrived, peers, others, scatter_cross, scatter_sems
    )
    greet(ring, (ring.next(), ring.previous(), ring.mate), 2)

    early, late = (PACK, Q, K, V), (O, INNER)

    def hops(group, step):
        if 1 <= step < chips:
            for i in group:
                gather.hop(i, step)

    def crosses(group, step):
        if 1 <= step < chips:
            for i in group:
                gather.cross(i, step)

    def row(name):
        return vec[VECTOR[name] : VECTOR[name] + 1, :]

    def by_blocks(step):
        def go(block, carry):
            step(pl.ds(pl.multiple_of(block * BLOCK, BLOCK), BLOCK))
            return carry

        lax.fori_loop(0, frame_count // BLOCK, go, 0)

    def by_columns(start, stop, step, size=CHUNK):
        def go(chunk, carry):
            step(chunk)
            return carry

        lax.fori_loop(start, stop, go, 0)

    def columns(chunk, size=CHUNK):
        return pl.ds(pl.multiple_of(chunk * size, size), size)

    def add_row(index, value):
        gvec[index : index + 1, :] += value

    def sum_rows(value):
        return jnp.sum(value, axis=0, keepdims=True)

    groups = ((early, 0), (late, LAG_LATE), ((OUTER,), LAG_OUTER))

    def gather_tick(tick):
        for group, lag in groups:
            if tick == lag:
                for i in group:
                    gather.start(i)
            hops(group, tick - lag)
            crosses(group, tick - lag - 1)

    gather_tick(0)

    gvec[...] = jnp.zeros_like(gvec)
    place[...] = place_table(shards, narrow, width)

    def start_norm(at):
        value = frames[at, :].astype(jnp.float32)
        centered = value - jnp.mean(value, axis=-1, keepdims=True)
        inv = lax.rsqrt(jnp.mean(centered * centered, axis=-1, keepdims=True) + EPSILON)
        inv_one[at, :] = inv
        hat_one[at, :] = centered * inv
        add_row(VECTOR[14], sum_rows(cotangent[at, :].astype(jnp.float32)))

    by_blocks(start_norm)

    for tick in range(1, chips + 1):
        gather_tick(tick)
    for i in early:
        gather.finish(i)

    picks = pick_table(shards, ratio)
    spread = dot_nt(weights[PACK][...], place[...])
    spread = jnp.where(group_mask(shards, ratio, narrow, width), spread, 0.0)
    vec[...] = matmul(picks, spread.astype(jnp.bfloat16))

    ticks = [functools.partial(gather_tick, t) for t in range(chips + 1, chips + LAG_OUTER + 1)]
    late_ticks = LAG_LATE
    served = [0]

    def serve_gather(number):
        for _ in range(number):
            if served[0] < len(ticks):
                ticks[served[0]]()
                served[0] += 1

    streams = []

    def serve(number):
        for _ in range(number):
            for stream in streams:
                if stream:
                    stream.pop(0)()

    def first_norm(at):
        value = hat_one[at, :] * row(0) + row(1)
        first[at, :] = value.astype(jnp.bfloat16)

    by_blocks(first_norm)

    def project(i, target, bias, scale):
        def go(chunk):
            at = columns(chunk)
            value = matmul(first[...], weights[i][:, at])
            if bias is not None:
                value = value + vec[VECTOR[bias] : VECTOR[bias] + 1, at]
            target[:, at] = (value * scale).astype(jnp.bfloat16)

        by_columns(0, width // CHUNK, go)

    project(Q, query, 3, HD ** (-0.5))
    serve_gather(SERVE[0])
    project(K, keys, None, 1.0)
    serve_gather(SERVE[1])
    project(V, values, 6, 1.0)
    serve_gather(SERVE[2])

    pair_width = 2 * HD
    pairs = width // pair_width
    lower = iota((1, pair_width), 1) < HD
    halves = (one_hot(lower), one_hot(jnp.logical_not(lower)))

    def attend(pair):
        at = pl.ds(pair * pair_width, pair_width)
        q_pair, k_pair, v_pair = query[:, at], keys[:, at], values[:, at]
        parts = []
        for half in range(2):
            scores = dot_nt(q_pair * halves[half], k_pair)
            grown = jnp.exp(scores - jnp.max(scores, axis=-1, keepdims=True))
            prob = (grown / jnp.sum(grown, axis=-1, keepdims=True)).astype(jnp.bfloat16)
            probs[2 * pair + half] = prob
            parts.append(matmul(prob, v_pair))
        context[:, at] = jnp.where(lower, parts[0], parts[1]).astype(jnp.bfloat16)

    for pair in range(pairs):
        attend(pair)
        serve_gather(pair % 2)
    serve_gather(late_ticks - served[0])
    for i in late:
        gather.finish(i)

    def mix(chunk):
        at = columns(chunk)
        value = matmul(context[...], weights[O][:, at])
        bias = vec[VECTOR[8] : VECTOR[8] + 1, at]
        mixed[:, at] = frames[:, at].astype(jnp.float32) + value + bias

    by_columns(0, width // CHUNK, mix)

    def second_norm(at):
        value = mixed[at, :]
        centered = value - jnp.mean(value, axis=-1, keepdims=True)
        inv = lax.rsqrt(jnp.mean(centered * centered, axis=-1, keepdims=True) + EPSILON)
        hat = centered * inv
        inv_two[at, :] = inv
        hat_two[at, :] = hat
        second[at, :] = (hat * row(9) + row(10)).astype(jnp.bfloat16)

    by_blocks(second_norm)
    serve_gather(1)

    per_row = width // CHUNK

    def inner_step(line, chunk):
        inside = columns(chunk)
        at = columns(line * per_row + chunk)
        value = matmul(second[...], weights[INNER][:, at])
        value = value + vec[SPREAD + line : SPREAD + line + 1, inside]
        gelu, grad = gelu_parts(value)
        active[:, at] = gelu.astype(jnp.bfloat16)
        slope[:, at] = grad.astype(jnp.bfloat16)

    for line in range(ratio):
        by_columns(0, per_row, functools.partial(inner_step, line))
        serve_gather(1)

    def outer_grad(chunk):
        at = columns(chunk)
        terms[OUTER][at, :] = dot_tn(active[:, at], cotangent[...]).astype(jnp.bfloat16)

    for line in range(ratio):
        by_columns(line * per_row, (line + 1) * per_row, outer_grad)
        serve_gather(1)
    scatter.start(OUTER)
    serve_gather(len(ticks))
    gather.finish(OUTER)

    def scatter_tick(group, step):
        for i in group:
            if step == 0:
                scatter.give(i, 0)
            if step + 1 < chips:
                scatter.give(i, step + 1)
            scatter.hop(i, step)

    def plan(group):
        streams.append([functools.partial(scatter_tick, group, t) for t in range(chips)])

    def waiting():
        return max(len(stream) for stream in streams)

    def inner_grad(line, chunk):
        inside = columns(chunk)
        at = columns(line * per_row + chunk)
        value = dot_nt(cotangent[...], weights[OUTER][at, :]) * slope[:, at].astype(jnp.float32)
        gvec[SPREAD + line : SPREAD + line + 1, inside] = sum_rows(value)
        low = value.astype(jnp.bfloat16)
        d_inner[:, at] = low
        terms[INNER][:, at] = dot_tn(second[...], low).astype(jnp.bfloat16)

    plan((OUTER,))
    for line in range(ratio):
        by_columns(0, per_row, functools.partial(inner_grad, line))
        serve(PACE_INNER[line % len(PACE_INNER)])
    scatter.start(INNER)
    plan((INNER,))

    def second_back(chunk):
        at = columns(chunk)
        total[:, at] = dot_nt(d_inner[...], weights[INNER][at, :])

    by_columns(0, width // CHUNK, second_back)
    serve(PACE[0])

    def norm_step(grad_ref, hat_ref, inv_ref, gain, shift, at):
        grad, hat = grad_ref[at, :], hat_ref[at, :]
        add_row(VECTOR[gain], sum_rows(grad * hat))
        add_row(VECTOR[shift], sum_rows(grad))
        return norm_back(grad, hat, inv_ref[at, :], row(gain))

    def mixed_back(at):
        back = norm_step(total, hat_two, inv_two, 9, 10, at)
        value = cotangent[at, :].astype(jnp.float32) + back
        add_row(VECTOR[8], sum_rows(value))
        total[at, :] = value
        second[at, :] = value.astype(jnp.bfloat16)

    by_blocks(mixed_back)
    serve(PACE[1])

    def context_back(chunk):
        at = columns(chunk)
        d_context[:, at] = dot_nt(second[...], weights[O][at, :]).astype(jnp.bfloat16)

    by_columns(0, width // CHUNK, context_back)
    serve(PACE[2])

    def square_grad(i, left, right, chunk):
        at = columns(chunk)
        terms[i][at, :] = dot_tn(left[:, at], right[...]).astype(jnp.bfloat16)

    def grad_of(i, left, right):
        by_columns(0, width // CHUNK, functools.partial(square_grad, i, left, right))
        scatter.start(i)

    grad_of(O, context, second)
    plan((O,))
    serve(PACE[3])

    def attend_back(pair):
        at = pl.ds(pair * pair_width, pair_width)
        q_pair, k_pair, v_pair = query[:, at], keys[:, at], values[:, at]
        d_pair = d_context[:, at]
        product = d_pair.astype(jnp.float32) * context[:, at].astype(jnp.float32)
        d_q, d_k, d_v = [], [], []
        for half in range(2):
            prob = probs[2 * pair + half]
            inside = lower if half == 0 else jnp.logical_not(lower)
            delta = jnp.sum(jnp.where(inside, product, 0.0), axis=-1, keepdims=True)
            d_prob = dot_nt(d_pair * halves[half], v_pair)
            d_score = (prob.astype(jnp.float32) * (d_prob - delta)).astype(jnp.bfloat16)
            d_v.append(dot_tn(prob, d_pair))
            d_q.append(matmul(d_score, k_pair))
            d_k.append(dot_tn(d_score, q_pair))
        d_query = jnp.where(lower, d_q[0], d_q[1]) * HD ** (-0.5)
        d_values = jnp.where(lower, d_v[0], d_v[1])
        gvec[VECTOR[3] : VECTOR[3] + 1, at] = sum_rows(d_query)
        gvec[VECTOR[6] : VECTOR[6] + 1, at] = sum_rows(d_values)
        query[:, at] = d_query.astype(jnp.bfloat16)
        keys[:, at] = jnp.where(lower, d_k[0], d_k[1]).astype(jnp.bfloat16)
        values[:, at] = d_values.astype(jnp.bfloat16)

    for pair in range(pairs):
        attend_back(pair)
        serve(PACE_PAIR[pair % len(PACE_PAIR)])
    grad_of(V, first, values)
    plan((V,))
    serve(PACE[4])
    grad_of(K, first, keys)
    plan((K,))
    serve(PACE[5])
    grad_of(Q, first, query)
    plan((Q,))
    serve(PACE[6])

    def first_back(chunk):
        at = columns(chunk)
        hat_two[:, at] = (
            dot_nt(query[...], weights[Q][at, :])
            + dot_nt(keys[...], weights[K][at, :])
            + dot_nt(values[...], weights[V][at, :])
        )

    by_columns(0, width // CHUNK, first_back)
    serve(PACE[7])

    def start_back(at):
        back = norm_step(hat_two, hat_one, inv_one, 0, 1, at)
        d_start[at, :] = (total[at, :] + back).astype(jnp.bfloat16)

    by_blocks(start_back)
    lines = dot_tn(picks, gvec[...].astype(jnp.bfloat16))
    lines = jnp.where(group_mask(shards, ratio, narrow, width), lines, 0.0)
    terms[PACK][...] = matmul(lines.astype(jnp.bfloat16), place[...]).astype(jnp.bfloat16)
    scatter.start(PACK)
    plan((PACK,))
    serve(PACE[8])

    def finish_result(chunk):
        at = columns(chunk)
        value = mixed[:, at] + matmul(active[...], weights[OUTER][:, at])
        bias = vec[VECTOR[14] : VECTOR[14] + 1, at]
        result[:, at] = (value + bias).astype(jnp.bfloat16)

    by_columns(0, width // CHUNK, finish_result)
    serve(waiting())
    for i in (OUTER, INNER, O, V, K, Q, PACK):
        scatter.finish(i)
    for i in range(count):
        gather.drain(i)
        scatter.drain(i)


LAG_LATE = 0
LAG_OUTER = 2
SERVE = (1, 1, 1)
PACE_INNER = (0, 1)
PACE = (0, 0, 1, 0, 0, 0, 0, 1, 0)
PACE_PAIR = (0, 0, 1)


def crossings(sizes, names, share):
    cut = [size // share for size in sizes]
    return tuple(c if i in names and c % SUBLANES == 0 else 0 for i, c in enumerate(cut))


def layer(frames, cotangent, pieces, shards):
    chips, (rows, width) = shards // 2, frames.shape
    hidden = pieces[INNER].shape[1]
    sizes = [piece.shape[0] for piece in pieces]
    wides = [piece.shape[1] for piece in pieces]
    gather_cross = crossings(sizes, range(6), 3)
    thirds = crossings(sizes, (V, O, INNER), 3)
    quarters = crossings(sizes, (OUTER,), 4)
    scatter_cross = tuple(a + b for a, b in zip(thirds, quarters))
    full = [(size * shards, wide) for size, wide in zip(sizes, wides)]
    ringed = [(size - cross, wide) for size, cross, wide in zip(sizes, scatter_cross, wides)]
    low, high = jnp.bfloat16, jnp.float32
    dma = pltpu.SemaphoreType.DMA
    scratch = (
        [pltpu.VMEM(shape, low) for shape in full] * 2
        + [pltpu.VMEM((chips, size, wide), low) for size, wide in zip(sizes, wides)]
        + [pltpu.VMEM((chips - 1,) + shape, low) for shape in ringed]
        + [pltpu.VMEM(shape, low) for shape in ringed]
        + [
            pltpu.VMEM((chips, cross, wide), low)
            for cross, wide in zip(scatter_cross, wides)
            if cross
        ]
        + [
            pltpu.VMEM((rows, width), high),
            pltpu.VMEM((rows, 1), high),
            pltpu.VMEM((rows, width), low),
            pltpu.VMEM((rows, width), low),
            pltpu.VMEM((rows, width), low),
            pltpu.VMEM((rows, width), low),
            pltpu.VMEM((width // HD, rows, rows), low),
            pltpu.VMEM((rows, width), low),
            pltpu.VMEM((rows, width), high),
            pltpu.VMEM((rows, width), high),
            pltpu.VMEM((rows, 1), high),
            pltpu.VMEM((rows, width), low),
            pltpu.VMEM((rows, hidden), low),
            pltpu.VMEM((rows, hidden), low),
            pltpu.VMEM((rows, hidden), low),
            pltpu.VMEM((rows, width), high),
            pltpu.VMEM((rows, width), low),
            pltpu.VMEM((SLOTS, width), high),
            pltpu.VMEM((SLOTS, width), high),
            pltpu.VMEM((width, LANES), low),
        ]
        + [dma((chips, 7))] * 6
        + [dma((7,))]
        + [dma((chips, 7))] * 6
        + [dma((7,))] * 2
    )
    vmem = pl.BlockSpec(memory_space=pltpu.VMEM)
    return pl.pallas_call(
        functools.partial(layer_kernel, shards, gather_cross, scatter_cross),
        out_shape=[jax.ShapeDtypeStruct((rows, width), low)] * 2
        + [jax.ShapeDtypeStruct(shape, high) for shape in zip(sizes, wides)],
        in_specs=[vmem] * 2 + [pl.BlockSpec(memory_space=pl.ANY)] * 7,
        out_specs=[vmem] * 9,
        scratch_shapes=scratch,
        compiler_params=pltpu.CompilerParams(
            collective_id=2, has_side_effects=True, vmem_limit_bytes=67043328
        ),
        name="layer",
    )(frames, cotangent, *pieces)


def fits(shards, reps, frames, local):
    narrow, wide = local[0].shape[0], local[WIDE].shape[0]
    return (
        reps == 2
        and shards >= 4
        and shards & (shards - 1) == 0
        and frames.shape[0] == 1
        and frames.shape[1] % CHUNK == 0
        and frames.shape[2] % CHUNK == 0
        and all(local[i].shape[0] % (3 * SUBLANES) == 0 for i in WEIGHTS)
        and wide % narrow == 0
        and SPREAD + wide // narrow <= SLOTS
        and narrow <= LANES
    )


def per_device(shards, reps, frames, cotangent, *local):
    if not fits(shards, reps, frames, local):
        return per_device_plain(shards, reps, frames, cotangent, *local)
    narrow, wide = local[0].shape[0], local[WIDE].shape[0]
    ratio = wide // narrow
    pieces = [local[i] for i in WEIGHTS] + [pack_local(local, narrow, ratio)]
    result, d_start, *sums = layer(frames[0], cotangent[0], pieces, shards)
    out = [None] * len(local)
    for k, i in enumerate(WEIGHTS):
        out[i] = sums[k]
    for k, i in enumerate(NARROW):
        out[i] = sums[PACK][k, :narrow]
    out[WIDE] = sums[PACK][SPREAD : SPREAD + ratio, :narrow].reshape(-1)
    return (result[None], d_start[None], *out)


def solution(mesh):
    clips = P(("shard", "rep"), None, None)
    weights = tuple(P("shard", None) if i in WEIGHTS else P("shard") for i in range(15))
    return jax.shard_map(
        functools.partial(per_device, mesh.shape["shard"], mesh.shape["rep"]),
        mesh=mesh,
        in_specs=(clips, clips) + weights,
        out_specs=(clips, clips) + weights,
        check_vma=False,
    )
```
